256 devices in a mesh: seq: 32 (over x, y, core), head: 8 (over z).
Axes of the slice: x: 4, y: 4, z: 8, core: 2. Of those that a mesh axis runs over, the one named last changes fastest.
Arguments:
- queries: bfloat16 [12288, 3072], P('seq', 'head'), may hold values from -8 to 8
- key_states: bfloat16 [12288, 3072], P('seq', 'head'), may hold values from -8 to 8
- value_states: bfloat16 [12288, 3072], P('seq', 'head'), may hold values from -6 to 6
- block_lists: int32 [96, 4], replicated, may hold values from 0 to 95, as said below
- out_weight: bfloat16 [3072, 3072], P('head'), may hold values from -0.15625 to 0.15625
- out_grad: bfloat16 [12288, 3072], P('seq', 'head'), may hold values from -6 to 6
Outputs:
- attended: bfloat16 [12288, 3072], P('seq', 'head')
- query_grad: bfloat16 [12288, 3072], P('seq', 'head')
- key_grad: bfloat16 [12288, 3072], P('seq', 'head')
- value_grad: bfloat16 [12288, 3072], P('seq', 'head')
The draws below stay inside these ranges and needn't reach their ends.
Inputs may be any that keep to these rules, and one draw needn't show every extreme that they name: `block_lists`: row r names 4 different blocks, among them block r itself; 2 of them lie in r's own group of 3 blocks and 2 in other groups. Of each group's blocks at most two are named by rows of other groups, and the rows of one group name at most one block of any other group.
All inputs are finite; a program needn't handle non-finite values.
Results may differ from the reference program's by a relative error of at most 0.035.
Values may be sent and summed in bfloat16 or wider, within the bound.
No kernel may reach another device: no remote copies, remote signals or barrier semaphores. Data moves between devices by JAX's collectives and lax.ppermute only.
A program may use at most 192 MiB of HBM per device.

```python
import math
import jax
import jax.numpy as jnp
from jax import lax

D = 3072
HEADS = 24
HD = 128
BLK = 128
LOCQ = 2
REMQ = 2
K_SEL = 4
QB_DEV = 3
GROUPS = 32
NQB = 96
CELLS = 12288
N_HEAD = 8


def base_rows(key, salt):
    noise_key = jax.random.fold_in(key, salt)
    return jnp.clip(1.6 * jax.random.normal(noise_key, (CELLS, HEADS * HD), jnp.float32), -8.0, 8.0)


def draw_queries(key, part):
    row_values = base_rows(key, 11)
    return row_values.astype(jnp.bfloat16)


def draw_key_states(key, part):
    row_values = base_rows(key, 12)
    return row_values.astype(jnp.bfloat16)


def draw_block_lists(key, part):
    port_key = jax.random.fold_in(key, 201)
    pick_key = jax.random.fold_in(key, 202)
    remote_key = jax.random.fold_in(key, 203)
    local_key = jax.random.fold_in(key, 204)
    special_key = jax.random.fold_in(key, 205)
    forced_key = jax.random.fold_in(key, 206)
    order_key = jax.random.fold_in(key, 207)
    first_port = jax.random.randint(port_key, (GROUPS,), 0, QB_DEV)
    second_port = (first_port + jax.random.randint(jax.random.fold_in(port_key, 1), (GROUPS,), 1, QB_DEV)) % QB_DEV
    port_pairs = jnp.stack([first_port, second_port], axis=1).astype(jnp.int32)
    group_ids = jnp.arange(GROUPS, dtype=jnp.int32)
    port_picks = jax.random.randint(pick_key, (GROUPS, GROUPS), 0, 2).astype(jnp.int32)
    port_picks = port_picks.at[group_ids, (group_ids + 1) % GROUPS].set(0)
    port_picks = port_picks.at[group_ids, (group_ids + 2) % GROUPS].set(1)
    row_ids = jnp.arange(NQB, dtype=jnp.int32)
    groups_of = row_ids // QB_DEV
    inner_index = row_ids % QB_DEV
    special = jax.random.randint(special_key, (GROUPS,), 0, QB_DEV).astype(jnp.int32)
    drawn_steps = jax.vmap(lambda sub_key: jax.random.permutation(sub_key, GROUPS - 1)[:REMQ] + 1)(jax.random.split(remote_key, NQB)).astype(jnp.int32)
    forced_tail = jax.vmap(lambda sub_key: jax.random.permutation(sub_key, GROUPS - 3)[:REMQ - 2] + 3)(jax.random.split(forced_key, NQB)).astype(jnp.int32)
    forced = jnp.concatenate([jnp.broadcast_to(jnp.array([1, 2], jnp.int32), (NQB, 2)), forced_tail], axis=1)
    is_special = (inner_index == special[groups_of])[:, None]
    offsets = jnp.where(is_special, forced, drawn_steps)
    owners = (groups_of[:, None] + offsets) % GROUPS
    chosen = port_picks[groups_of[:, None], owners]
    far_blocks = owners * QB_DEV + port_pairs[owners, chosen]
    near_steps = jax.vmap(lambda sub_key: jax.random.permutation(sub_key, QB_DEV - 1)[:LOCQ - 1] + 1)(jax.random.split(local_key, NQB)).astype(jnp.int32)
    near_blocks = groups_of[:, None] * QB_DEV + (inner_index[:, None] + near_steps) % QB_DEV
    listed = jnp.concatenate([row_ids[:, None], near_blocks, far_blocks], axis=1)
    column_order = jax.vmap(lambda sub_key: jax.random.permutation(sub_key, K_SEL))(jax.random.split(order_key, NQB)).astype(jnp.int32)
    return jnp.take_along_axis(listed, column_order, axis=1).astype(jnp.int32)


def strengthened(values, stream_key, source, target, blocks, factor):
    def block_of(dim):
        return (jnp.arange(values.shape[dim]) // (values.shape[dim] // blocks)).reshape((-1,) + (1,) * (values.ndim - 1 - dim))

    one_side = jax.random.permutation(stream_key, blocks)[block_of(target)]
    other_side = (block_of(target) + blocks // 2) % blocks
    return jnp.where((block_of(source) == one_side) | (block_of(source) == other_side), factor * values, values)


def shard_levels(own_key, dims, cuts, low, largest):
    def one(dim, shards_of):
        heights = jax.random.uniform(jax.random.fold_in(jax.random.fold_in(own_key, 6), dim), (shards_of,), jnp.float32, low / len(cuts), largest / len(cuts))
        return jnp.repeat(jnp.exp(heights), dims[dim] // shards_of).reshape((-1,) + (1,) * (len(dims) - dim - 1))

    level = one(*cuts[0])
    for cut in cuts[1:]:
        level = level * one(*cut)
    return level


def normal_values(stream_key, shape, width, reach, cuts=(), kind=jnp.bfloat16):
    gain = shard_levels(stream_key, shape, cuts, -0.22, 0.18) if cuts else 1.0
    values = jax.random.normal(stream_key, shape, jnp.float32) * width * gain
    return jnp.minimum(jnp.maximum(values, -reach), reach).astype(kind)


def gaussian_with(key, extent, scale, limit, pieces, heavy, kind=jnp.bfloat16):
    values = scale * jax.random.normal(key, extent, jnp.float32)
    if pieces:
        values = values * shard_levels(key, extent, pieces, -0.22, 0.18)
    return jnp.clip(strengthened(values, jax.random.fold_in(key, 3), *heavy), -limit, limit).astype(kind)


def setup_inputs(seed: int = 0) -> dict:
    key_of = jax.random.split(jax.random.key(seed), 7)
    return {
        "queries": draw_queries(jax.random.fold_in(key_of[6], 71), 0),
        "key_states": draw_key_states(jax.random.fold_in(key_of[6], 71), 0),
        "value_states": normal_values(key_of[2], (CELLS, HEADS * HD), 1.0, 6.0, ((0, 32), (1, 8))),
        "block_lists": draw_block_lists(jax.random.fold_in(key_of[6], 71), 0),
        "out_weight": gaussian_with(key_of[4], (HEADS * HD, D), (HEADS * HD) ** -0.5, 0.15625, ((0, 8),), (0, 1, 8, 2.0)),
        "out_grad": normal_values(key_of[5], (CELLS, D), 1.0, 6.0, ((0, 32), (1, 8))),
    }


def log_total(scores):
    row_top = lax.optimization_barrier(jnp.max(scores, axis=-1, keepdims=True))
    return row_top + jnp.log(lax.optimization_barrier(jnp.sum(jnp.exp(scores - row_top), axis=-1, keepdims=True)))

def settle(values):
    return lax.optimization_barrier(values.astype(jnp.bfloat16)).astype(jnp.float32)

def reference(queries, key_states, value_states, block_lists, out_weight, out_grad):
    score_scale = 1.0 / math.sqrt(HD)
    feature_width = HEADS * HD
    grad_attn = jnp.dot(out_grad, out_weight.T, preferred_element_type=jnp.float32).astype(jnp.bfloat16)
    key_blocks = key_states.reshape(NQB, BLK, HEADS, HD)
    value_blocks = value_states.reshape(NQB, BLK, HEADS, HD)
    query_groups = queries.reshape(GROUPS, QB_DEV, BLK, HEADS, HD)
    grad_groups = grad_attn.reshape(GROUPS, QB_DEV, BLK, HEADS, HD)
    list_groups = block_lists.reshape(GROUPS, QB_DEV, K_SEL)
    block_owner = jnp.arange(NQB, dtype=jnp.int32) // QB_DEV
    entry_order = jnp.arange(QB_DEV * K_SEL, dtype=jnp.int32)

    def group_step(grad_total, inputs):
        group_index, query_rows, grad_rows, group_lists = inputs
        key_rows = key_blocks[group_lists].reshape(QB_DEV, K_SEL * BLK, HEADS, HD).astype(jnp.float32)
        value_rows = value_blocks[group_lists].reshape(QB_DEV, K_SEL * BLK, HEADS, HD).astype(jnp.float32)
        query_f = query_rows.astype(jnp.float32)
        grad_f = grad_rows.astype(jnp.float32)
        scores = jnp.einsum('bihd,bjhd->bhij', query_f, key_rows) * score_scale
        probs = jnp.exp(scores - log_total(scores))
        probs_low = settle(probs)
        attention = jnp.einsum('bhij,bjhd->bihd', probs_low, value_rows).astype(jnp.bfloat16)
        row_delta = jnp.einsum('bihd,bihd->bhi', grad_f, attention.astype(jnp.float32))[..., None]
        value_terms = jnp.einsum('bhij,bihd->bjhd', probs_low, grad_f)
        grad_prob = jnp.einsum('bihd,bjhd->bhij', grad_f, value_rows)
        grad_score = settle(probs * (grad_prob - row_delta))
        query_grad = (jnp.einsum('bhij,bjhd->bihd', grad_score, key_rows) * score_scale).astype(jnp.bfloat16)
        key_terms = jnp.einsum('bhij,bihd->bjhd', grad_score, query_f) * score_scale
        slot_terms = jnp.concatenate([key_terms.reshape(QB_DEV * K_SEL, BLK, feature_width), value_terms.reshape(QB_DEV * K_SEL, BLK, feature_width)], axis=2)
        flat_ids = group_lists.reshape(-1).astype(jnp.int32)
        same_block = flat_ids[:, None] == flat_ids[None, :]
        first_seen = jnp.logical_not(jnp.any(same_block & (entry_order[None, :] < entry_order[:, None]), axis=1))
        block_sums = jnp.zeros((NQB, BLK, 2 * feature_width), jnp.float32).at[flat_ids].add(slot_terms)
        grouped = block_sums[flat_ids]
        own_group = (block_owner[flat_ids] == group_index)[:, None, None]
        settled = jnp.where(own_group, grouped, settle(grouped))
        settled = jnp.where(first_seen[:, None, None], settled, jnp.zeros_like(settled))
        return (grad_total.at[flat_ids].add(settled), (attention, query_grad))
    zero_carry = jnp.zeros((NQB, BLK, 2 * feature_width), jnp.float32)
    grad_total, (attention, query_grad) = lax.scan(group_step, zero_carry, (jnp.arange(GROUPS, dtype=jnp.int32), query_groups, grad_groups, list_groups))
    attention = attention.reshape(CELLS, feature_width)
    part_width = feature_width // N_HEAD
    mixed_sum = jnp.zeros((CELLS, D), jnp.float32)
    for part_index in range(N_HEAD):
        low_edge = part_index * part_width
        part_product = jnp.dot(attention[:, low_edge:low_edge + part_width], out_weight[low_edge:low_edge + part_width], preferred_element_type=jnp.float32)
        mixed_sum = mixed_sum + settle(part_product)
    grad_total = grad_total.reshape(CELLS, 2 * feature_width)
    return (mixed_sum.astype(jnp.bfloat16), query_grad.reshape(CELLS, feature_width), grad_total[:, :feature_width].astype(jnp.bfloat16), grad_total[:, feature_width:].astype(jnp.bfloat16))
```

```python
import math

import jax
import jax.numpy as jnp
from jax import lax
from jax.experimental import pallas as pl
from jax.experimental.pallas import tpu as pltpu
from jax.sharding import PartitionSpec as P

HD = 128
BLK = 128
K_SEL = 4


SMEM = pl.BlockSpec(memory_space=pltpu.SMEM)
VMEM = pl.BlockSpec(memory_space=pltpu.VMEM)
ANY = pl.BlockSpec(memory_space=pl.ANY)
LIMIT = 56 * 1024 * 1024


def asked_of(lists, group, me, blocks):
    found = jnp.int32(-1)
    for item in range(blocks * K_SEL):
        entry = lists[group * (blocks * K_SEL) + item] - me * blocks
        found = jnp.where((entry >= 0) & (entry < blocks), entry, found)
    return jnp.where(group == me, -1, found)


def pack_body(groups, blocks, lists, me_ref, key, value, sent, sems):
    me = me_ref[0]

    def copies(group, block):
        rows = pl.ds(pl.multiple_of(block * BLK, BLK), BLK)
        return (
            pltpu.make_async_copy(key.at[rows], sent.at[group, 0], sems.at[group, 0]),
            pltpu.make_async_copy(value.at[rows], sent.at[group, 1], sems.at[group, 1]),
        )

    def start(group, carry):
        block = asked_of(lists, group, me, blocks)

        @pl.when(block >= 0)
        def _():
            for copy in copies(group, block):
                copy.start()

        return carry | jnp.where(block >= 0, jnp.int32(1) << group, 0)

    mask = lax.fori_loop(0, groups, start, jnp.int32(0))

    def finish(group, carry):
        @pl.when(((mask >> group) & 1) != 0)
        def _():
            for copy in copies(group, 0):
                copy.wait()

        return carry

    lax.fori_loop(0, groups, finish, 0)


def attend_body(
    blocks, heads, scale, lists, me_ref, query, key, value, grad, arrived,
    attention, query_grad, near, sent,
    key_rows, value_rows, totals, low, sems, out_sems,
):
    me = me_ref[0]
    width = heads * HD
    slot_of = []
    far_block = []
    far_slot = []
    for block in range(blocks):
        for item in range(K_SEL):
            entry = lists[(me * blocks + block) * K_SEL + item]
            place = entry - me * blocks
            local = (place >= 0) & (place < blocks)
            owner = entry // blocks
            rows = pl.ds(item * BLK, BLK)
            sem_k = sems.at[block, item, 0]
            sem_v = sems.at[block, item, 1]

            @pl.when(local)
            def _():
                source = pl.ds(pl.multiple_of(place * BLK, BLK), BLK)
                pltpu.make_async_copy(key.at[source], key_rows.at[block, rows], sem_k).start()
                pltpu.make_async_copy(value.at[source], value_rows.at[block, rows], sem_v).start()

            @pl.when(jnp.logical_not(local))
            def _():
                pltpu.make_async_copy(arrived.at[owner, 0], key_rows.at[block, rows], sem_k).start()
                pltpu.make_async_copy(arrived.at[owner, 1], value_rows.at[block, rows], sem_v).start()

            number = block * K_SEL + item
            own = jnp.int32(blocks + number)
            for earlier in range(number - 1, -1, -1):
                own = jnp.where(far_block[earlier] == entry, blocks + earlier, own)
            slot_of.append(jnp.where(local, place, own))
            far_block.append(entry)
            far_slot.append((jnp.logical_not(local) & (own == blocks + number), owner))
    totals[...] = jnp.zeros_like(totals)
    for block in range(blocks):
        for item in range(K_SEL):
            rows = pl.ds(item * BLK, BLK)
            pltpu.make_async_copy(key.at[pl.ds(0, BLK)], key_rows.at[block, rows], sems.at[block, item, 0]).wait()
            pltpu.make_async_copy(value.at[pl.ds(0, BLK)], value_rows.at[block, rows], sems.at[block, item, 1]).wait()
        own_rows = pl.ds(block * BLK, BLK)
        for head in range(heads):
            columns = pl.ds(head * HD, HD)
            q = query[own_rows, columns]
            g = grad[own_rows, columns]
            k = key_rows[block, :, columns]
            v = value_rows[block, :, columns]
            scores = lax.dot_general(q, k, (((1,), (1,)), ((), ())), preferred_element_type=jnp.float32) * scale
            top = jnp.max(scores, axis=-1, keepdims=True)
            raised = jnp.exp(scores - top)
            probs = raised * (1.0 / jnp.sum(raised, axis=-1, keepdims=True))
            probs_low = probs.astype(jnp.bfloat16)
            mixed = jnp.dot(probs_low, v, preferred_element_type=jnp.float32).astype(jnp.bfloat16)
            attention[own_rows, columns] = mixed
            delta = jnp.sum(g.astype(jnp.float32) * mixed.astype(jnp.float32), axis=-1, keepdims=True)
            grad_prob = lax.dot_general(g, v, (((1,), (1,)), ((), ())), preferred_element_type=jnp.float32)
            grad_score = (probs * (grad_prob - delta)).astype(jnp.bfloat16)
            query_grad[own_rows, columns] = (
                jnp.dot(grad_score, k, preferred_element_type=jnp.float32) * scale
            ).astype(jnp.bfloat16)
            key_terms = lax.dot_general(
                grad_score, q, (((0,), (0,)), ((), ())), preferred_element_type=jnp.float32
            ) * scale
            value_terms = lax.dot_general(
                probs_low, g, (((0,), (0,)), ((), ())), preferred_element_type=jnp.float32
            )
            for item in range(K_SEL):
                slot = slot_of[block * K_SEL + item]
                part = slice(item * BLK, (item + 1) * BLK)
                totals[slot, :, columns] += key_terms[part]
                totals[slot, :, pl.ds(width + head * HD, HD)] += value_terms[part]
    for number, (first, owner) in enumerate(far_slot):

        @pl.when(first)
        def _():
            low[number] = totals[blocks + number].astype(jnp.bfloat16)
            pltpu.make_async_copy(low.at[number], sent.at[owner], out_sems.at[number]).start()

    near[...] = totals[:blocks].reshape(blocks * BLK, 2 * width)
    for number, (first, owner) in enumerate(far_slot):

        @pl.when(first)
        def _():
            pltpu.make_async_copy(low.at[number], sent.at[owner], out_sems.at[number]).wait()


def collect_body(groups, blocks, lists, me_ref, near, returned, key_grad, value_grad, total, held, sems):
    me = me_ref[0]
    width = key_grad.shape[1]

    def start(group, carry):
        block = asked_of(lists, group, me, blocks)

        @pl.when(block >= 0)
        def _():
            pltpu.make_async_copy(returned.at[group], held.at[group], sems.at[group]).start()

        return tuple(
            mask | jnp.where(block == place, jnp.int32(1) << group, 0)
            for place, mask in enumerate(carry)
        )

    masks = lax.fori_loop(0, groups, start, (jnp.int32(0),) * blocks)
    total[...] = near[...]

    def finish(group, carry):
        for block in range(blocks):

            @pl.when(((masks[block] >> group) & 1) != 0)
            def _():
                pltpu.make_async_copy(returned.at[group], held.at[group], sems.at[group]).wait()
                total[pl.ds(block * BLK, BLK)] += held[group].astype(jnp.float32)

        return carry

    lax.fori_loop(0, groups, finish, 0)
    key_grad[...] = total[:, :width].astype(jnp.bfloat16)
    value_grad[...] = total[:, width:].astype(jnp.bfloat16)


def grad_body(size, me_ref, weight, *refs):
    pieces, out = refs[:size], refs[size]
    me = me_ref[0]
    width = out.shape[1]
    total = None
    for step, piece in enumerate(pieces):
        start = lax.rem(me + step, size) * width
        term = lax.dot_general(
            piece[...], weight[:, pl.ds(pl.multiple_of(start, HD), width)],
            (((1,), (1,)), ((), ())), preferred_element_type=jnp.float32,
        )
        total = term if total is None else total + term
    out[...] = total.astype(jnp.bfloat16)


def project_body(size, me_ref, attention, weight, *outs):
    me = me_ref[0]
    width = attention.shape[1]
    for step, out in enumerate(outs):
        start = lax.rem(me + step, size) * width
        out[...] = jnp.dot(
            attention[...], weight[:, pl.ds(pl.multiple_of(start, HD), width)],
            preferred_element_type=jnp.float32,
        ).astype(jnp.bfloat16)


def gather_ring(x, axis, size):
    ahead = [(i, (i + 1) % size) for i in range(size)]
    back = [(i, (i - 1) % size) for i in range(size)]
    pieces = [None] * size
    pieces[0] = x
    half = size // 2
    from_low, from_high = x, x
    for step in range(1, half):
        from_low = lax.ppermute(from_low, axis, ahead)
        from_high = lax.ppermute(from_high, axis, back)
        pieces[size - step] = from_low
        pieces[step] = from_high
    cut = x.shape[0] // 2
    pieces[half] = jnp.concatenate(
        [lax.ppermute(from_low[:cut], axis, ahead), lax.ppermute(from_high[cut:], axis, back)]
    )
    return pieces


def scatter_ring(parts, axis, size):
    ahead = [(i, (i + 1) % size) for i in range(size)]
    back = [(i, (i - 1) % size) for i in range(size)]
    half = size // 2
    cut = parts[0].shape[0] // 2

    def add(*terms):
        total = terms[0].astype(jnp.float32)
        for term in terms[1:]:
            total = total + term.astype(jnp.float32)
        return total.astype(jnp.bfloat16)

    up = lax.ppermute(parts[half][:cut], axis, ahead)
    down = lax.ppermute(parts[half][cut:], axis, back)
    for distance in range(half - 1, 0, -1):
        high, low = parts[distance], parts[size - distance]
        if distance == half - 1:
            high = jnp.concatenate([add(high[:cut], up), high[cut:]])
            low = jnp.concatenate([low[:cut], add(low[cut:], down)])
        else:
            high, low = add(high, up), add(low, down)
        up = lax.ppermute(high, axis, ahead)
        down = lax.ppermute(low, axis, back)
    return add(parts[0], up, down)


def local(queries, key_states, value_states, block_lists, out_weight, out_grad):
    groups = lax.axis_size("seq")
    size = lax.axis_size("head")
    cells, width = queries.shape
    blocks = cells // BLK
    heads = width // HD
    lists = block_lists.reshape(-1)
    me = lax.axis_index("seq").reshape(1).astype(jnp.int32)
    column = lax.axis_index("head").reshape(1).astype(jnp.int32)
    bf16, f32 = jnp.bfloat16, jnp.float32

    def shape(*dims, dtype=bf16):
        return jax.ShapeDtypeStruct(dims, dtype)

    params = pltpu.CompilerParams(vmem_limit_bytes=LIMIT)
    sent = pl.pallas_call(
        lambda *refs: pack_body(groups, blocks, *refs),
        name="pack",
        in_specs=[SMEM, SMEM, VMEM, VMEM],
        out_specs=ANY,
        out_shape=shape(groups, 2, BLK, width),
        scratch_shapes=[pltpu.SemaphoreType.DMA((groups, 2))],
        compiler_params=params,
    )(lists, me, key_states, value_states)
    arrived = lax.all_to_all(sent, "seq", split_axis=0, concat_axis=0, tiled=True)
    pieces = gather_ring(out_grad, "head", size)
    grad_attn = pl.pallas_call(
        lambda *refs: grad_body(size, *refs),
        name="gradattn",
        in_specs=[SMEM] + [VMEM] * (size + 1),
        out_specs=VMEM,
        out_shape=shape(cells, width),
        compiler_params=params,
    )(column, out_weight, *pieces)
    attention, query_grad, near, far = pl.pallas_call(
        lambda *refs: attend_body(blocks, heads, 1.0 / math.sqrt(HD), *refs),
        name="attend",
        in_specs=[SMEM, SMEM, VMEM, ANY, ANY, VMEM, ANY],
        out_specs=[VMEM, VMEM, VMEM, ANY],
        out_shape=[
            shape(cells, width), shape(cells, width), shape(cells, 2 * width, dtype=f32),
            shape(groups, BLK, 2 * width),
        ],
        scratch_shapes=[
            pltpu.VMEM((blocks, K_SEL * BLK, width), bf16),
            pltpu.VMEM((blocks, K_SEL * BLK, width), bf16),
            pltpu.VMEM((blocks + blocks * K_SEL, BLK, 2 * width), f32),
            pltpu.VMEM((blocks * K_SEL, BLK, 2 * width), bf16),
            pltpu.SemaphoreType.DMA((blocks, K_SEL, 2)),
            pltpu.SemaphoreType.DMA((blocks * K_SEL,)),
        ],
        compiler_params=params,
    )(lists, me, queries, key_states, value_states, grad_attn, arrived)
    returned = lax.all_to_all(far, "seq", split_axis=0, concat_axis=0, tiled=True)
    parts = pl.pallas_call(
        lambda *refs: project_body(size, *refs),
        name="project",
        in_specs=[SMEM, VMEM, VMEM],
        out_specs=[VMEM] * size,
        out_shape=[shape(cells, width)] * size,
        compiler_params=params,
    )(column, attention, out_weight)
    attended = scatter_ring(parts, "head", size)
    key_grad, value_grad = pl.pallas_call(
        lambda *refs: collect_body(groups, blocks, *refs),
        name="collect",
        in_specs=[SMEM, SMEM, VMEM, ANY],
        out_specs=[VMEM, VMEM],
        out_shape=[shape(cells, width), shape(cells, width)],
        scratch_shapes=[
            pltpu.VMEM((cells, 2 * width), f32),
            pltpu.VMEM((groups, BLK, 2 * width), bf16),
            pltpu.SemaphoreType.DMA((groups,)),
        ],
        compiler_params=params,
    )(lists, me, near, returned)
    return attended, query_grad, key_grad, value_grad


def solution(mesh):
    in_specs = (
        P("seq", "head"),
        P("seq", "head"),
        P("seq", "head"),
        P(),
        P("head", None),
        P("seq", "head"),
    )
    out_specs = (P("seq", "head"), P("seq", "head"), P("seq", "head"), P("seq", "head"))
    return jax.shard_map(local, mesh=mesh, in_specs=in_specs, out_specs=out_specs, check_vma=False)
```

```python
import math

import jax
import jax.numpy as jnp
from jax import lax
from jax.experimental import pallas as pl
from jax.experimental.pallas import tpu as pltpu
from jax.sharding import PartitionSpec as P

HD = 128
BLK = 128
K_SEL = 4


SMEM = pl.BlockSpec(memory_space=pltpu.SMEM)
VMEM = pl.BlockSpec(memory_space=pltpu.VMEM)
ANY = pl.BlockSpec(memory_space=pl.ANY)


NX, NY, NC = 4, 4, 2


def place_of(group):
    return group // (NY * NC), (group // NC) % NY, group % NC


def steps_of(leg, sign):
    pairs = []
    for group in range(NX * NY * NC):
        x, y, core = place_of(group)
        if (core == 0) == (leg == 0):
            x = (x + sign) % NX
        else:
            y = (y + sign) % NY
        pairs.append((group, (x * NY + y) * NC + core))
    return pairs


def swap_of():
    return [(group, group ^ 1) for group in range(NX * NY * NC)]


def hop(x, leg, sign):
    return lax.ppermute(x, "seq", steps_of(leg, sign))


def route(me, entry, port, blocks):
    x, y, core = place_of(me)
    owner_x, owner_y, owner_core = place_of(entry // blocks)
    dx = (owner_x - x + NX) % NX
    dy = (owner_y - y + NY) % NY
    first = jnp.where(core == 0, dx, dy)
    second = jnp.where(core == 0, dy, dx)
    order = jnp.where(first == 0, 0, jnp.where(first == 3, 1, jnp.where(first == 1, 2, 3)))
    return second, order * 4 + 2 * jnp.where(owner_core == core, 0, 1) + port


def fetch(gathered, me, entry, port, blocks, target, sem):
    mid, low, high, far_low, far_high = gathered
    distance, index = route(me, entry, port, blocks)
    cases = (
        (distance == 0, mid, 0), (distance == 3, low, 0), (distance == 1, high, 0),
        ((distance == 2) & (index < 8), far_low, 0), ((distance == 2) & (index >= 8), far_high, 8),
    )
    for case, source, base in cases:

        @pl.when(case)
        def _():
            pltpu.make_async_copy(source.at[index - base], target, sem).start()


def pack_body(blocks, lists, me_ref, key, value, mine, other):
    me = me_ref[0]
    core = me % NC

    def scan(row, carry):
        named = carry
        for item in range(K_SEL):
            place = lists[row, item] - me * blocks
            hit = (place >= 0) & (place < blocks) & (row // blocks != me)
            named = named | jnp.where(hit, jnp.int32(1) << jnp.clip(place, 0, blocks - 1), 0)
        return named

    named = lax.fori_loop(0, lists.shape[0], scan, jnp.int32(0), unroll=8)
    first = jnp.where((named & 1) != 0, 0, jnp.where((named & 2) != 0, 1, 2))
    second = jnp.where((named & 4) != 0, 2, jnp.where((named & 2) != 0, 1, 0))
    for port, block in enumerate((first, second)):
        rows = pl.ds(pl.multiple_of(block * BLK, BLK), BLK)

        @pl.when(core == 0)
        def _():
            mine[port] = key[rows]
            other[port] = value[rows]

        @pl.when(core != 0)
        def _():
            mine[port] = value[rows]
            other[port] = key[rows]


def pick_body(blocks, lists, ports, me_ref, mid, low, high, far_low, far_high, out, sems):
    me = me_ref[0]
    partner = me + 1 - 2 * (me % NC)
    gathered = (mid, low, high, far_low, far_high)

    def start(step, count):
        block, item = step // K_SEL, step % K_SEL
        entry = lists[partner * blocks + block, item]
        place = entry - partner * blocks
        far = (place < 0) | (place >= blocks)
        count = jnp.where(item == 0, 0, count)
        number = jnp.minimum(2 * block + count, 2 * blocks - 1)

        @pl.when(far)
        def _():
            fetch(gathered, me, entry, ports[entry], blocks, out.at[number], sems.at[number])

        return count + jnp.where(far, 1, 0)

    lax.fori_loop(0, blocks * K_SEL, start, jnp.int32(0))
    for number in range(2 * blocks):
        pltpu.make_async_copy(mid.at[0], out.at[number], sems.at[number]).wait()


def attend_body(
    blocks, heads, scale, lists, ports, me_ref, query, key, value, grad, swapped,
    mid, low, high, far_low, far_high,
    attention, query_grad, near, mine, other,
    rows_of, totals, slots, sems,
):
    me = me_ref[0]
    core = me % NC
    width = heads * HD
    gathered = (mid, low, high, far_low, far_high)

    def start(step, count):
        block, item = step // K_SEL, step % K_SEL
        entry = lists[me * blocks + block, item]
        place = entry - me * blocks
        far = (place < 0) | (place >= blocks)
        count = jnp.where(item == 0, 0, count)
        order = jnp.minimum(2 * block + count, 2 * blocks - 1)
        rows = pl.ds(pl.multiple_of(item * BLK, BLK), BLK)

        @pl.when(jnp.logical_not(far))
        def _():
            source = pl.ds(pl.multiple_of(place * BLK, BLK), BLK)
            pltpu.make_async_copy(key.at[source], rows_of.at[0, block, rows], sems.at[block, item, 0]).start()
            pltpu.make_async_copy(value.at[source], rows_of.at[1, block, rows], sems.at[block, item, 1]).start()

        @pl.when(far)
        def _():
            fetch(gathered, me, entry, ports[entry], blocks, rows_of.at[core, block, rows], sems.at[block, item, core])
            pltpu.make_async_copy(
                swapped.at[order], rows_of.at[1 - core, block, rows], sems.at[block, item, 1 - core]
            ).start()

        slot = jnp.where(far, blocks + order, place)
        for earlier in range(blocks * K_SEL):
            same = (earlier < step) & (lists[me * blocks + earlier // K_SEL, earlier % K_SEL] == entry)
            slot = jnp.where(same, jnp.minimum(slot, slots[earlier]), slot)
        slots[step] = slot
        return count + jnp.where(far, 1, 0)

    for step in range(blocks * K_SEL):
        slots[step] = 0
    lax.fori_loop(0, blocks * K_SEL, start, jnp.int32(0))
    totals[...] = jnp.zeros_like(totals)
    @pl.loop(0, blocks)
    def _(block):
        for item in range(K_SEL):
            rows = pl.ds(item * BLK, BLK)
            for kind in range(2):
                pltpu.make_async_copy(
                    key.at[pl.ds(0, BLK)], rows_of.at[kind, block, rows], sems.at[block, item, kind]
                ).wait()
        own_rows = pl.ds(pl.multiple_of(block * BLK, BLK), BLK)
        for head in range(heads):
            columns = pl.ds(head * HD, HD)
            q = query[own_rows, columns]
            g = grad[own_rows, columns]
            k = rows_of[0, block, :, columns]
            v = rows_of[1, block, :, columns]
            scores = lax.dot_general(q, k, (((1,), (1,)), ((), ())), preferred_element_type=jnp.float32) * scale
            top = jnp.max(scores, axis=-1, keepdims=True)
            raised = jnp.exp(scores - top)
            probs = raised * (1.0 / jnp.sum(raised, axis=-1, keepdims=True))
            probs_low = probs.astype(jnp.bfloat16)
            mixed = jnp.dot(probs_low, v, preferred_element_type=jnp.float32).astype(jnp.bfloat16)
            attention[own_rows, columns] = mixed
            delta = jnp.sum(g.astype(jnp.float32) * mixed.astype(jnp.float32), axis=-1, keepdims=True)
            grad_prob = lax.dot_general(g, v, (((1,), (1,)), ((), ())), preferred_element_type=jnp.float32)
            grad_score = (probs * (grad_prob - delta)).astype(jnp.bfloat16)
            query_grad[own_rows, columns] = (
                jnp.dot(grad_score, k, preferred_element_type=jnp.float32) * scale
            ).astype(jnp.bfloat16)
            key_terms = lax.dot_general(
                grad_score, q, (((0,), (0,)), ((), ())), preferred_element_type=jnp.float32
            ) * scale
            value_terms = lax.dot_general(
                probs_low, g, (((0,), (0,)), ((), ())), preferred_element_type=jnp.float32
            )
            for item in range(K_SEL):
                slot = slots[block * K_SEL + item]
                part = slice(item * BLK, (item + 1) * BLK)
                totals[0, slot, :, columns] += key_terms[part]
                totals[1, slot, :, columns] += value_terms[part]

    mine[...] = totals[core, blocks:].astype(jnp.bfloat16)
    other[...] = totals[1 - core, blocks:].astype(jnp.bfloat16)
    near[...] = totals[:, :blocks].reshape(2, blocks * BLK, width)


def add_terms(blocks, lists, ports, me, mine, theirs, cases):
    partner = me + 1 - 2 * (me % NC)
    for group, terms in ((me, mine), (partner, theirs)):

        def body(step, count):
            block, item = step // K_SEL, step % K_SEL
            entry = lists[group * blocks + block, item]
            place = entry - group * blocks
            far = (place < 0) | (place >= blocks)
            count = jnp.where(item == 0, 0, count)
            number = jnp.minimum(2 * block + count, 2 * blocks - 1)
            distance, index = route(me, entry, ports[entry], blocks)
            for second, low, high, ref in cases:

                @pl.when(far & (distance == second) & (index >= low) & (index < high))
                def _():
                    ref[index - low] = (
                        ref[index - low].astype(jnp.float32) + terms[number].astype(jnp.float32)
                    ).astype(ref.dtype)

            return count + jnp.where(far, 1, 0)

        lax.fori_loop(0, blocks * K_SEL, body, jnp.int32(0))


def far_body(blocks, lists, ports, me_ref, mine, theirs, far_low, far_high):
    far_low[...] = jnp.zeros_like(far_low)
    far_high[...] = jnp.zeros_like(far_high)
    add_terms(blocks, lists, ports, me_ref[0], mine, theirs, ((2, 0, 8, far_low), (2, 8, 16, far_high)))


def side_body(blocks, lists, ports, me_ref, mine, theirs, from_low, from_high, up, down):
    up[:8] = from_low[...]
    up[8:] = jnp.zeros_like(from_low)
    down[:8] = jnp.zeros_like(from_high)
    down[8:] = from_high[...]
    add_terms(blocks, lists, ports, me_ref[0], mine, theirs, ((1, 0, 16, up), (3, 0, 16, down)))


def mid_body(blocks, lists, ports, me_ref, mine, theirs, from_low, from_high, own, down, up, far_low, far_high, total):
    total[...] = from_low[...].astype(jnp.float32) + from_high[...].astype(jnp.float32)
    add_terms(blocks, lists, ports, me_ref[0], mine, theirs, ((0, 0, 16, total),))
    own[...] = total[0:4].astype(jnp.bfloat16)
    down[...] = total[4:8].astype(jnp.bfloat16)
    up[...] = total[8:12].astype(jnp.bfloat16)
    far_low[...] = total[12:14].astype(jnp.bfloat16)
    far_high[...] = total[14:16].astype(jnp.bfloat16)


def turn_body(down, up, from_low, from_high, down_out, up_out):
    f32 = jnp.float32
    up_out[:2] = (up[:2].astype(f32) + from_low[...].astype(f32)).astype(jnp.bfloat16)
    up_out[2:] = up[2:]
    down_out[:2] = down[:2]
    down_out[2:] = (down[2:].astype(f32) + from_high[...].astype(f32)).astype(jnp.bfloat16)


def sum_body(own, from_low, from_high, mine, other):
    f32 = jnp.float32
    total = (own[...].astype(f32) + from_low[...].astype(f32) + from_high[...].astype(f32)).astype(jnp.bfloat16)
    mine[...] = total[:2]
    other[...] = total[2:]


def collect_body(blocks, ports, named, me_ref, near, mine, swapped, key_grad, value_grad):
    me = me_ref[0]
    core = me % NC
    f32 = jnp.float32
    for block in range(blocks):
        rows = pl.ds(block * BLK, BLK)
        port = ports[me * blocks + block]
        weight = named[me * blocks + block] != 0
        for kind, out in enumerate((key_grad, value_grad)):
            term = jnp.where(core == kind, mine[port].astype(f32), swapped[port].astype(f32))
            out[rows] = (near[kind, rows] + jnp.where(weight, term, 0.0)).astype(jnp.bfloat16)


def grad_body(size, me_ref, weight, *refs):
    pieces, out = refs[:size], refs[size]
    me = me_ref[0]
    width = out.shape[1]
    total = None
    for step, piece in enumerate(pieces):
        start = lax.rem(me + step, size) * width
        term = lax.dot_general(
            piece[...], weight[:, pl.ds(pl.multiple_of(start, HD), width)],
            (((1,), (1,)), ((), ())), preferred_element_type=jnp.float32,
        )
        total = term if total is None else total + term
    out[...] = total.astype(jnp.bfloat16)


def project_body(size, me_ref, attention, weight, *outs):
    me = me_ref[0]
    width = attention.shape[1]
    for step, out in enumerate(outs):
        start = lax.rem(me + step, size) * width
        out[...] = jnp.dot(
            attention[...], weight[:, pl.ds(pl.multiple_of(start, HD), width)],
            preferred_element_type=jnp.float32,
        ).astype(jnp.bfloat16)


def add(*terms):
    total = terms[0].astype(jnp.float32)
    for term in terms[1:]:
        total = total + term.astype(jnp.float32)
    return total.astype(jnp.bfloat16)


def ring_hop(x, sign):
    size = lax.axis_size("head")
    return lax.ppermute(x, "head", [(i, (i + sign) % size) for i in range(size)])


def ring_pair(pair):
    return ring_hop(pair[0], 1), ring_hop(pair[1], -1)


def together(*values):
    return lax.optimization_barrier(values)


def local(queries, key_states, value_states, block_lists, out_weight, out_grad):
    size = lax.axis_size("head")
    cells, width = queries.shape
    blocks = cells // BLK
    heads = width // HD
    me = lax.axis_index("seq").reshape(1).astype(jnp.int32)
    column = lax.axis_index("head").reshape(1).astype(jnp.int32)
    bf16, f32 = jnp.bfloat16, jnp.float32
    far = 2 * blocks

    def shape(*dims, dtype=bf16):
        return jax.ShapeDtypeStruct(dims, dtype)

    def call(body, name, in_specs, out_shape, *operands, mib=16, scratch=()):
        return pl.pallas_call(
            body,
            name=name,
            in_specs=in_specs,
            out_specs=[VMEM] * len(out_shape),
            out_shape=out_shape,
            scratch_shapes=scratch,
            compiler_params=pltpu.CompilerParams(vmem_limit_bytes=mib * 1024 * 1024),
        )(*operands)

    piece = shape(2, BLK, width)
    mine, other = call(
        lambda *refs: pack_body(blocks, *refs), "pack", [SMEM, SMEM, VMEM, VMEM], [piece, piece],
        block_lists, me, key_states, value_states,
    )
    entries = block_lists.reshape(-1)
    entry_group = jnp.arange(entries.shape[0], dtype=jnp.int32) // (blocks * K_SEL)
    far_entry = jnp.where(entries // blocks != entry_group, entries, -1)
    all_blocks = jnp.arange(block_lists.shape[0], dtype=jnp.int32)
    named = jnp.any(far_entry[None, :] == all_blocks[:, None], axis=1).astype(jnp.int32)
    ahead = jnp.concatenate([jnp.zeros((1,), jnp.int32), named[:-1]])
    ahead2 = jnp.concatenate([jnp.zeros((2,), jnp.int32), named[:-2]])
    inner = all_blocks % blocks
    ports = jnp.where(inner == 0, 0, jnp.where(inner == 1, ahead, jnp.maximum(ahead, ahead2)))

    half = size // 2
    cut = cells // 2
    ring = [(out_grad, out_grad), ring_pair((out_grad, out_grad))]
    base = jnp.concatenate([mine, lax.ppermute(other, "seq", swap_of())])
    base, held = together(base, ring[1])
    left, right = hop(base, 0, 1), hop(base, 0, -1)
    ring.append(ring_pair(held))
    over_low, over_high = hop(left[:2], 0, 1), hop(right[2:], 0, -1)
    mid = jnp.concatenate([base, left, right, over_low, over_high])
    mid, held = together(mid, ring[2])
    low, high = hop(mid, 1, 1), hop(mid, 1, -1)
    ring.append(ring_pair(held))
    next_low, next_high, held = together(low[:8], high[8:], (ring[3][0][:cut], ring[3][1][cut:]))
    far_low, far_high = hop(next_low, 1, 1), hop(next_high, 1, -1)
    pieces = [out_grad] + [None] * (size - 1)
    for step in range(1, half):
        pieces[size - step], pieces[step] = ring[step]
    pieces[half] = jnp.concatenate(ring_pair(held))
    gathered = (mid, low, high, far_low, far_high)
    (picked,) = call(
        lambda *refs: pick_body(blocks, *refs), "pick", [SMEM, SMEM, SMEM] + [ANY] * 5, [shape(far, BLK, width)],
        block_lists, ports, me, *gathered, scratch=[pltpu.SemaphoreType.DMA((far,))],
    )
    swapped = lax.ppermute(picked, "seq", swap_of())

    (grad_attn,) = call(
        lambda *refs: grad_body(size, *refs), "gradattn", [SMEM] + [VMEM] * (size + 1), [shape(cells, width)],
        column, out_weight, *pieces,
    )
    attention, query_grad, near, terms, terms_other = call(
        lambda *refs: attend_body(blocks, heads, 1.0 / math.sqrt(HD), *refs), "attend",
        [SMEM, SMEM, SMEM, VMEM, ANY, ANY, VMEM] + [ANY] * 6,
        [
            shape(cells, width), shape(cells, width), shape(2, cells, width, dtype=f32),
            shape(far, BLK, width), shape(far, BLK, width),
        ],
        block_lists, ports, me, queries, key_states, value_states, grad_attn, swapped, *gathered,
        scratch=[
            pltpu.VMEM((2, blocks, K_SEL * BLK, width), bf16),
            pltpu.VMEM((2, blocks + far, BLK, width), f32),
            pltpu.SMEM((blocks * K_SEL,), jnp.int32),
            pltpu.SemaphoreType.DMA((blocks, K_SEL, 2)),
        ],
        mib=24,
    )
    theirs = lax.ppermute(terms_other, "seq", swap_of())
    parts = call(
        lambda *refs: project_body(size, *refs), "project", [SMEM, VMEM, VMEM], [shape(cells, width)] * size,
        column, attention, out_weight,
    )
    terms, theirs, parts = together(terms, theirs, parts)
    lead = (block_lists, ports, me, terms, theirs)
    lead_specs = [SMEM, SMEM, SMEM, VMEM, VMEM]
    far_low, far_high = call(
        lambda *refs: far_body(blocks, *refs), "far", lead_specs, [shape(8, BLK, width)] * 2, *lead
    )
    ahead, back = ring_pair((parts[half][:cut], parts[half][cut:]))
    up, down = call(
        lambda *refs: side_body(blocks, *refs), "side", lead_specs + [VMEM] * 2, [shape(16, BLK, width)] * 2,
        *lead, hop(far_low, 1, 1), hop(far_high, 1, -1),
    )
    ahead = jnp.concatenate([add(parts[half - 1][:cut], ahead), parts[half - 1][cut:]])
    back = jnp.concatenate([parts[half + 1][:cut], add(parts[half + 1][cut:], back)])
    up, down, held = together(up, down, (ahead, back))
    from_low, from_high = hop(up, 1, 1), hop(down, 1, -1)
    ahead, back = ring_pair(held)
    ahead, back = ring_pair((add(parts[2], ahead), add(parts[size - 2], back)))
    own, down, up, far_low, far_high = call(
        lambda *refs: mid_body(blocks, *refs), "mid", lead_specs + [VMEM] * 2,
        [shape(4, BLK, width)] * 3 + [piece] * 2, *lead, from_low, from_high,
        scratch=[pltpu.VMEM((16, BLK, width), f32)],
    )
    far_low, far_high, held = together(
        far_low, far_high, (add(parts[1], ahead), add(parts[size - 1], back))
    )
    from_low, from_high = hop(far_low, 0, 1), hop(far_high, 0, -1)
    ahead, back = ring_pair(held)
    attended = add(parts[0], ahead, back)
    down, up = call(
        turn_body, "turn", [VMEM] * 4, [shape(4, BLK, width)] * 2, down, up, from_low, from_high,
    )
    mine, other = call(
        sum_body, "sum", [VMEM] * 3, [piece, piece], own, hop(up, 0, 1), hop(down, 0, -1)
    )
    key_grad, value_grad = call(
        lambda *refs: collect_body(blocks, *refs), "collect", [SMEM, SMEM, SMEM] + [VMEM] * 3,
        [shape(cells, width)] * 2,
        ports, named, me, near, mine, lax.ppermute(other, "seq", swap_of()),
    )
    return attended, query_grad, key_grad, value_grad


def solution(mesh):
    in_specs = (
        P("seq", "head"),
        P("seq", "head"),
        P("seq", "head"),
        P(),
        P("head", None),
        P("seq", "head"),
    )
    out_specs = (P("seq", "head"), P("seq", "head"), P("seq", "head"), P("seq", "head"))
    return jax.shard_map(local, mesh=mesh, in_specs=in_specs, out_specs=out_specs, check_vma=False)
```

```python
import math

import jax
import jax.numpy as jnp
from jax import lax
from jax.experimental import pallas as pl
from jax.experimental.pallas import tpu as pltpu
from jax.sharding import PartitionSpec as P


HD = 128
BLK = 128
K_SEL = 4


SMEM = pl.BlockSpec(memory_space=pltpu.SMEM)
VMEM = pl.BlockSpec(memory_space=pltpu.VMEM)
ANY = pl.BlockSpec(memory_space=pl.ANY)


NX, NY, NC = 4, 4, 2


def place_of(group):
    return group // (NY * NC), (group // NC) % NY, group % NC


def steps_of(leg, sign):
    pairs = []
    for group in range(NX * NY * NC):
        x, y, core = place_of(group)
        if (core == 0) == (leg == 0):
            x = (x + sign) % NX
        else:
            y = (y + sign) % NY
        pairs.append((group, (x * NY + y) * NC + core))
    return pairs


def swap_of():
    return [(group, group ^ 1) for group in range(NX * NY * NC)]


def hop(x, leg, sign):
    return lax.ppermute(x, "seq", steps_of(leg, sign))


def swap(x):
    return lax.ppermute(x, "seq", swap_of())


def route(me, entry, port, blocks):
    x, y, core = place_of(me)
    owner_x, owner_y, owner_core = place_of(entry // blocks)
    dx = (owner_x - x + NX) % NX
    dy = (owner_y - y + NY) % NY
    first = jnp.where(core == 0, dx, dy)
    second = jnp.where(core == 0, dy, dx)
    order = jnp.where(first == 0, 0, jnp.where(first == 3, 1, jnp.where(first == 1, 2, 3)))
    return second, order * 4 + 2 * jnp.where(owner_core == core, 0, 1) + port


def fetch(gathered, code, target, sem):
    for kind, source in enumerate(gathered):

        @pl.when(code // 16 == kind)
        def _():
            pltpu.make_async_copy(source.at[code % 16], target, sem).start()


def pack_body(blocks, lists, me_ref, key, value, mine, other, sems):
    me = me_ref[0]
    core = me % NC
    row = lax.broadcasted_iota(jnp.int32, lists.shape, 0) - me * blocks
    entry = jnp.where((row < 0) | (row >= blocks), lists[...] - me * blocks, -1)
    named = [jnp.max(jnp.where(entry == block, 1.0, 0.0)) > 0.5 for block in range(blocks)]
    first = jnp.where(named[0], 0, jnp.where(named[1], 1, 2))
    second = jnp.where(named[2], 2, jnp.where(named[1], 1, 0))
    for port, block in enumerate((first, second)):
        rows = pl.ds(pl.multiple_of(block * BLK, BLK), BLK)

        @pl.when(core == 0)
        def _():
            pltpu.make_async_copy(key.at[rows], mine.at[port], sems.at[port, 0]).start()
            pltpu.make_async_copy(value.at[rows], other.at[port], sems.at[port, 1]).start()

        @pl.when(core != 0)
        def _():
            pltpu.make_async_copy(value.at[rows], mine.at[port], sems.at[port, 0]).start()
            pltpu.make_async_copy(key.at[rows], other.at[port], sems.at[port, 1]).start()

    for port in range(2):
        rows = pl.ds(0, BLK)
        pltpu.make_async_copy(key.at[rows], mine.at[port], sems.at[port, 0]).wait()
        pltpu.make_async_copy(key.at[rows], other.at[port], sems.at[port, 1]).wait()


def plan_body(blocks, lists, ports, me_ref, table, orders):
    me = me_ref[0]
    far_count = 2 * blocks
    steps = blocks * K_SEL
    partner = me + 1 - 2 * (me % NC)
    for group_index, group in enumerate((me, partner)):

        def body(step, count):
            block, item = step // K_SEL, step % K_SEL
            entry = lists[group * blocks + block, item]
            place = entry - group * blocks
            far = (place < 0) | (place >= blocks)
            count = jnp.where(item == 0, 0, count)
            number = jnp.minimum(2 * block + count, far_count - 1)
            distance, index = route(me, entry, ports[entry], blocks)
            kind = jnp.where(index < 8, 0, 4) + jnp.where(
                distance == 0, 0, jnp.where(distance == 3, 1, jnp.where(distance == 1, 2, 3))
            )
            first = number
            for earlier in range(steps):
                same = (earlier < step) & (lists[group * blocks + earlier // K_SEL, earlier % K_SEL] == entry)
                first = jnp.where(same, jnp.minimum(first, orders[earlier]), first)
            orders[step] = number

            @pl.when(far)
            def _():
                table[group_index * far_count + number] = kind * 16 + index % 8
                table[(2 + group_index) * far_count + number] = jnp.where(first == number, 1, 0)

            if group_index == 0:
                table[4 * far_count + step] = jnp.where(far, blocks + first, place)
                table[4 * far_count + steps + step] = jnp.where(far, number, -1)
            return count + jnp.where(far, 1, 0)

        for step in range(steps):
            orders[step] = far_count
        lax.fori_loop(0, steps, body, jnp.int32(0))


def pick_body(far_count, table, *refs):
    gathered, out, sems = refs[:-2], refs[-2], refs[-1]
    for number in range(far_count):
        fetch(gathered, table[far_count + number], out.at[number], sems.at[number])
    for number in range(far_count):
        pltpu.make_async_copy(gathered[0].at[0], out.at[number], sems.at[number]).wait()


def attend_body(blocks, heads, scale, table, me_ref, query, key, value, grad, swapped, *refs):
    gathered, refs = refs[:8], refs[8:]
    attention, query_grad, near, mine, other, rows_of, totals, sems = refs
    me = me_ref[0]
    core = me % NC
    width = heads * HD
    far_count = 2 * blocks
    steps = blocks * K_SEL

    def start(step, carry):
        block, item = step // K_SEL, step % K_SEL
        slot = table[4 * far_count + step]
        number = table[4 * far_count + steps + step]
        rows = pl.ds(pl.multiple_of(item * BLK, BLK), BLK)

        @pl.when(number < 0)
        def _():
            source = pl.ds(pl.multiple_of(slot * BLK, BLK), BLK)
            pltpu.make_async_copy(key.at[source], rows_of.at[0, block, rows], sems.at[block, item, 0]).start()
            pltpu.make_async_copy(value.at[source], rows_of.at[1, block, rows], sems.at[block, item, 1]).start()

        @pl.when(number >= 0)
        def _():
            fetch(gathered, table[jnp.maximum(number, 0)], rows_of.at[core, block, rows], sems.at[block, item, core])
            pltpu.make_async_copy(
                swapped.at[jnp.maximum(number, 0)], rows_of.at[1 - core, block, rows], sems.at[block, item, 1 - core]
            ).start()

        return carry

    lax.fori_loop(0, steps, start, 0)
    totals[...] = jnp.zeros_like(totals)

    @pl.loop(0, blocks)
    def _(block):
        for item in range(K_SEL):
            rows = pl.ds(item * BLK, BLK)
            for kind in range(2):
                pltpu.make_async_copy(
                    key.at[pl.ds(0, BLK)], rows_of.at[kind, block, rows], sems.at[block, item, kind]
                ).wait()
        own_rows = pl.ds(pl.multiple_of(block * BLK, BLK), BLK)
        for head in range(heads):
            columns = pl.ds(head * HD, HD)
            q = query[own_rows, columns]
            g = grad[own_rows, columns]
            k = rows_of[0, block, :, columns]
            v = rows_of[1, block, :, columns]
            scores = lax.dot_general(q, k, (((1,), (1,)), ((), ())), preferred_element_type=jnp.float32) * scale
            top = jnp.max(scores, axis=-1, keepdims=True)
            raised = jnp.exp(scores - top)
            probs = raised * (1.0 / jnp.sum(raised, axis=-1, keepdims=True))
            probs_low = probs.astype(jnp.bfloat16)
            mixed = jnp.dot(probs_low, v, preferred_element_type=jnp.float32).astype(jnp.bfloat16)
            attention[own_rows, columns] = mixed
            delta = jnp.sum(g.astype(jnp.float32) * mixed.astype(jnp.float32), axis=-1, keepdims=True)
            grad_prob = lax.dot_general(g, v, (((1,), (1,)), ((), ())), preferred_element_type=jnp.float32)
            grad_score = (probs * (grad_prob - delta)).astype(jnp.bfloat16)
            query_grad[own_rows, columns] = (
                jnp.dot(grad_score, k, preferred_element_type=jnp.float32) * scale
            ).astype(jnp.bfloat16)
            key_terms = lax.dot_general(
                grad_score, q, (((0,), (0,)), ((), ())), preferred_element_type=jnp.float32
            ) * scale
            value_terms = lax.dot_general(
                probs_low, g, (((0,), (0,)), ((), ())), preferred_element_type=jnp.float32
            )
            for item in range(K_SEL):
                slot = table[4 * far_count + block * K_SEL + item]
                part = slice(item * BLK, (item + 1) * BLK)
                totals[0, slot, :, columns] += key_terms[part]
                totals[1, slot, :, columns] += value_terms[part]

    mine[...] = totals[core, blocks:].astype(jnp.bfloat16)
    other[...] = totals[1 - core, blocks:].astype(jnp.bfloat16)
    near[...] = totals[:, :blocks].reshape(2, blocks * BLK, width)


def add_terms(table, mine, theirs, cases):
    far_count = mine.shape[0]
    for group, terms in enumerate((mine, theirs)):

        def body(number, carry):
            code = table[group * far_count + number]
            first = table[(2 + group) * far_count + number] != 0
            for kind, ref in cases:

                @pl.when(first & (code // 16 == kind))
                def _():
                    index = code % 16

                    @pl.loop(0, 4)
                    def _(part):
                        rows = pl.ds(pl.multiple_of(part * (BLK // 4), BLK // 4), BLK // 4)
                        ref[index, rows] = (
                            ref[index, rows].astype(jnp.float32) + terms[number, rows].astype(jnp.float32)
                        ).astype(ref.dtype)

            return carry

        lax.fori_loop(0, far_count, body, 0)


def early_body(table, mine, theirs, far_low, far_high, up, down):
    for ref in (far_low, far_high, up, down):
        ref[...] = jnp.zeros_like(ref)
    add_terms(table, mine, theirs, ((3, far_low), (7, far_high), (6, up), (1, down)))


def late_body(table, mine, theirs, from_low, from_high, up, down):
    up[...] = from_low[...]
    down[...] = from_high[...]
    add_terms(table, mine, theirs, ((2, up), (5, down)))


def mid_body(table, mine, theirs, low_first, high_first, low_second, high_second, own, down, up, far_low, far_high, first, second):
    f32, bf16 = jnp.float32, jnp.bfloat16
    first[...] = low_first[...].astype(f32) + high_first[...].astype(f32)
    second[...] = low_second[...].astype(f32) + high_second[...].astype(f32)
    add_terms(table, mine, theirs, ((0, first), (4, second)))
    own[...] = first[0:4].astype(bf16)
    down[...] = first[4:8].astype(bf16)
    up[...] = second[0:4].astype(bf16)
    far_low[...] = second[4:6].astype(bf16)
    far_high[...] = second[6:8].astype(bf16)


def turn_body(down, up, from_low, from_high, down_out, up_out):
    f32 = jnp.float32
    up_out[:2] = (up[:2].astype(f32) + from_low[...].astype(f32)).astype(jnp.bfloat16)
    up_out[2:] = up[2:]
    down_out[:2] = down[:2]
    down_out[2:] = (down[2:].astype(f32) + from_high[...].astype(f32)).astype(jnp.bfloat16)


def sum_body(own, from_low, from_high, mine, other):
    f32 = jnp.float32
    total = (own[...].astype(f32) + from_low[...].astype(f32) + from_high[...].astype(f32)).astype(jnp.bfloat16)
    mine[...] = total[:2]
    other[...] = total[2:]


def collect_body(blocks, ports, named, me_ref, near, mine, swapped, key_grad, value_grad):
    me = me_ref[0]
    core = me % NC
    f32 = jnp.float32
    for block in range(blocks):
        rows = pl.ds(block * BLK, BLK)
        port = ports[me * blocks + block]
        weight = named[me * blocks + block] != 0
        for kind, out in enumerate((key_grad, value_grad)):
            term = jnp.where(core == kind, mine[port].astype(f32), swapped[port].astype(f32))
            out[rows] = (near[kind, rows] + jnp.where(weight, term, 0.0)).astype(jnp.bfloat16)


def grad_body(size, me_ref, weight, *refs):
    pieces, out = refs[:size], refs[size]
    me = me_ref[0]
    width = out.shape[1]

    @pl.loop(0, out.shape[0] // BLK)
    def _(block):
        rows = pl.ds(pl.multiple_of(block * BLK, BLK), BLK)
        total = None
        for step, piece in enumerate(pieces):
            start = lax.rem(me + step, size) * width
            term = lax.dot_general(
                piece[rows], weight[:, pl.ds(pl.multiple_of(start, HD), width)],
                (((1,), (1,)), ((), ())), preferred_element_type=jnp.float32,
            )
            total = term if total is None else total + term
        out[rows] = total.astype(jnp.bfloat16)


def project_body(size, me_ref, attention, weight, *outs):
    me = me_ref[0]
    width = attention.shape[1]

    @pl.loop(0, attention.shape[0] // BLK)
    def _(block):
        rows = pl.ds(pl.multiple_of(block * BLK, BLK), BLK)
        for step, out in enumerate(outs):
            start = lax.rem(me + step, size) * width
            out[rows] = jnp.dot(
                attention[rows], weight[:, pl.ds(pl.multiple_of(start, HD), width)],
                preferred_element_type=jnp.float32,
            ).astype(jnp.bfloat16)


def add(*terms):
    total = terms[0].astype(jnp.float32)
    for term in terms[1:]:
        total = total + term.astype(jnp.float32)
    return total.astype(jnp.bfloat16)


def ring_pair(pair):
    size = lax.axis_size("head")
    out = []
    for x, sign in ((pair[0], 1), (pair[1], -1)):
        out.append(lax.ppermute(x, "head", [(i, (i + sign) % size) for i in range(size)]))
    return tuple(out)


def layer(queries, key_states, value_states, block_lists, out_weight, out_grad):
    size = lax.axis_size("head")
    cells, width = queries.shape
    blocks = cells // BLK
    heads = width // HD
    me = lax.axis_index("seq").reshape(1).astype(jnp.int32)
    column = lax.axis_index("head").reshape(1).astype(jnp.int32)
    bf16, f32 = jnp.bfloat16, jnp.float32
    far = 2 * blocks

    def shape(*dims, dtype=bf16):
        return jax.ShapeDtypeStruct(dims, dtype)

    def call(body, in_specs, out_shape, *operands, out_specs=None, mib=16, scratch=()):
        return pl.pallas_call(
            body,
            in_specs=in_specs,
            out_specs=out_specs or [VMEM] * len(out_shape),
            out_shape=out_shape,
            scratch_shapes=scratch,
            compiler_params=pltpu.CompilerParams(vmem_limit_bytes=mib * 1024 * 1024),
        )(*operands)

    piece = shape(2, BLK, width)
    mine, other = call(
        lambda *refs: pack_body(blocks, *refs), [VMEM, SMEM, ANY, ANY], [piece, piece],
        block_lists, me, key_states, value_states, scratch=[pltpu.SemaphoreType.DMA((2, 2))], mib=60,
    )
    entries = block_lists.reshape(-1)
    entry_group = jnp.arange(entries.shape[0], dtype=jnp.int32) // (blocks * K_SEL)
    far_entry = jnp.where(entries // blocks != entry_group, entries, -1)
    all_blocks = jnp.arange(block_lists.shape[0], dtype=jnp.int32)
    named = jnp.any(far_entry[None, :] == all_blocks[:, None], axis=1).astype(jnp.int32)
    ahead = jnp.concatenate([jnp.zeros((1,), jnp.int32), named[:-1]])
    ahead2 = jnp.concatenate([jnp.zeros((2,), jnp.int32), named[:-2]])
    inner = all_blocks % blocks
    ports = jnp.where(inner == 0, 0, jnp.where(inner == 1, ahead, jnp.maximum(ahead, ahead2)))

    (table,) = call(
        lambda *refs: plan_body(blocks, *refs), [SMEM] * 3,
        [shape(4 * far + 2 * blocks * K_SEL, dtype=jnp.int32)], block_lists, ports, me,
        out_specs=[SMEM], scratch=[pltpu.SMEM((blocks * K_SEL,), jnp.int32)],
    )

    half = size // 2
    cut = cells // 2
    ring = [(out_grad, out_grad)]
    for _ in range(1, half):
        ring.append(ring_pair(ring[-1]))
    pieces = [out_grad] + [None] * (size - 1)
    for step in range(1, half):
        pieces[size - step], pieces[step] = ring[step]
    pieces[half] = jnp.concatenate(ring_pair((ring[-1][0][:cut], ring[-1][1][cut:])))

    base = jnp.concatenate([mine, swap(other)])
    left, right = hop(base, 0, 1), hop(base, 0, -1)
    mid_a = jnp.concatenate([base, left])
    low_a, high_a = hop(mid_a, 1, 1), hop(mid_a, 1, -1)
    mid_b = jnp.concatenate([right, hop(left[:2], 0, 1), hop(right[2:], 0, -1)])
    low_b, high_b = hop(mid_b, 1, 1), hop(mid_b, 1, -1)
    far_a, far_b = hop(low_a, 1, 1), hop(high_b, 1, -1)
    gathered = (mid_a, low_a, high_a, far_a, mid_b, low_b, high_b, far_b)
    (picked,) = call(
        lambda *refs: pick_body(far, *refs), [SMEM] + [ANY] * 8, [shape(far, BLK, width)],
        table, *gathered, scratch=[pltpu.SemaphoreType.DMA((far,))],
    )
    swapped = swap(picked)
    (grad_attn,) = call(
        lambda *refs: grad_body(size, *refs), [SMEM] + [VMEM] * (size + 1), [shape(cells, width)],
        column, out_weight, *pieces,
    )
    attention, query_grad, near, terms, terms_other = call(
        lambda *refs: attend_body(blocks, heads, 1.0 / math.sqrt(HD), *refs),
        [SMEM, SMEM, VMEM, ANY, ANY, VMEM] + [ANY] * 9,
        [
            shape(cells, width), shape(cells, width), shape(2, cells, width, dtype=f32),
            shape(far, BLK, width), shape(far, BLK, width),
        ],
        table, me, queries, key_states, value_states, grad_attn, swapped, *gathered,
        scratch=[
            pltpu.VMEM((2, blocks, K_SEL * BLK, width), bf16),
            pltpu.VMEM((2, blocks + far, BLK, width), f32),
            pltpu.SemaphoreType.DMA((blocks, K_SEL, 2)),
        ],
        mib=24,
    )
    theirs = swap(terms_other)
    parts = call(
        lambda *refs: project_body(size, *refs), [SMEM, VMEM, VMEM], [shape(cells, width)] * size,
        column, attention, out_weight,
    )
    lead = (table, terms, theirs)
    lead_specs = [SMEM, VMEM, VMEM]
    eight = shape(8, BLK, width)
    far_low, far_high, up_b, down_a = call(early_body, lead_specs, [eight] * 4, *lead)
    from_low, from_high = hop(far_low, 1, 1), hop(far_high, 1, -1)
    low_b, high_a = hop(up_b, 1, 1), hop(down_a, 1, -1)
    ahead, back = ring_pair((parts[half][:cut], parts[half][cut:]))
    up_a, down_b = call(late_body, lead_specs + [VMEM] * 2, [eight] * 2, *lead, from_low, from_high)
    low_a, high_b = hop(up_a, 1, 1), hop(down_b, 1, -1)
    ahead = jnp.concatenate([add(parts[half - 1][:cut], ahead), parts[half - 1][cut:]])
    back = jnp.concatenate([parts[half + 1][:cut], add(parts[half + 1][cut:], back)])
    for distance in range(half - 2, -1, -1):
        ahead, back = ring_pair((ahead, back))
        if distance:
            ahead, back = add(parts[distance], ahead), add(parts[size - distance], back)
    attended = add(parts[0], ahead, back)
    own, down, up, far_low, far_high = call(
        mid_body, lead_specs + [VMEM] * 4, [shape(4, BLK, width)] * 3 + [piece] * 2,
        *lead, low_a, high_a, low_b, high_b,
        scratch=[pltpu.VMEM((8, BLK, width), f32)] * 2,
    )
    down, up = call(
        turn_body, [VMEM] * 4, [shape(4, BLK, width)] * 2,
        down, up, hop(far_low, 0, 1), hop(far_high, 0, -1),
    )
    mine, other = call(sum_body, [VMEM] * 3, [piece, piece], own, hop(up, 0, 1), hop(down, 0, -1))
    key_grad, value_grad = call(
        lambda *refs: collect_body(blocks, *refs), [SMEM, SMEM, SMEM] + [VMEM] * 3,
        [shape(cells, width)] * 2,
        ports, named, me, near, mine, swap(other),
    )
    return attended, query_grad, key_grad, value_grad


def solution(mesh):
    in_specs = (
        P("seq", "head"),
        P("seq", "head"),
        P("seq", "head"),
        P(),
        P("head", None),
        P("seq", "head"),
    )
    out_specs = (P("seq", "head"), P("seq", "head"), P("seq", "head"), P("seq", "head"))
    return jax.shard_map(layer, mesh=mesh, in_specs=in_specs, out_specs=out_specs, check_vma=False)
```

```python
import math

import jax
import jax.numpy as jnp
from jax import lax
from jax.experimental import pallas as pl
from jax.experimental.pallas import tpu as pltpu
from jax.sharding import PartitionSpec as P


HD = 128
BLK = 128
K_SEL = 4


SMEM = pl.BlockSpec(memory_space=pltpu.SMEM)
VMEM = pl.BlockSpec(memory_space=pltpu.VMEM)
ANY = pl.BlockSpec(memory_space=pl.ANY)


NX, NY, NC = 4, 4, 2


def place_of(group):
    return group // (NY * NC), (group // NC) % NY, group % NC


def steps_of(leg, sign):
    pairs = []
    for group in range(NX * NY * NC):
        x, y, core = place_of(group)
        if (core == 0) == (leg == 0):
            x = (x + sign) % NX
        else:
            y = (y + sign) % NY
        pairs.append((group, (x * NY + y) * NC + core))
    return pairs


def swap_of():
    return [(group, group ^ 1) for group in range(NX * NY * NC)]


def hop(x, leg, sign):
    return lax.ppermute(x, "seq", steps_of(leg, sign))


def swap(x):
    return lax.ppermute(x, "seq", swap_of())


def route(me, entry, port, blocks):
    x, y, core = place_of(me)
    owner_x, owner_y, owner_core = place_of(entry // blocks)
    dx = (owner_x - x + NX) % NX
    dy = (owner_y - y + NY) % NY
    first = jnp.where(core == 0, dx, dy)
    second = jnp.where(core == 0, dy, dx)
    order = jnp.where(first == 0, 0, jnp.where(first == 3, 1, jnp.where(first == 1, 2, 3)))
    return second, order * 4 + 2 * jnp.where(owner_core == core, 0, 1) + port


def fetch(gathered, code, target, sem):
    for kind, source in enumerate(gathered):

        @pl.when(code // 16 == kind)
        def _():
            pltpu.make_async_copy(source.at[code % 16], target, sem).start()


def join_body(*refs):
    out, start = refs[-1], 0
    for ref in refs[:-1]:
        out[start:start + ref.shape[0]] = ref[...]
        start += ref.shape[0]


def pack_body(blocks, lists, me_ref, key, value, mine, other, sems):
    me = me_ref[0]
    core = me % NC
    row = lax.broadcasted_iota(jnp.int32, lists.shape, 1) - me * blocks
    entry = jnp.where((row < 0) | (row >= blocks), lists[...] - me * blocks, -1)
    named = [jnp.max(jnp.where(entry == block, 1.0, 0.0)) > 0.5 for block in range(blocks)]
    first = jnp.where(named[0], 0, jnp.where(named[1], 1, 2))
    second = jnp.where(named[2], 2, jnp.where(named[1], 1, 0))
    for port, block in enumerate((first, second)):
        rows = pl.ds(pl.multiple_of(block * BLK, BLK), BLK)

        @pl.when(core == 0)
        def _():
            pltpu.make_async_copy(key.at[rows], mine.at[port], sems.at[port, 0]).start()
            pltpu.make_async_copy(value.at[rows], other.at[port], sems.at[port, 1]).start()

        @pl.when(core != 0)
        def _():
            pltpu.make_async_copy(value.at[rows], mine.at[port], sems.at[port, 0]).start()
            pltpu.make_async_copy(key.at[rows], other.at[port], sems.at[port, 1]).start()

    for port in range(2):
        rows = pl.ds(0, BLK)
        pltpu.make_async_copy(key.at[rows], mine.at[port], sems.at[port, 0]).wait()
        pltpu.make_async_copy(key.at[rows], other.at[port], sems.at[port, 1]).wait()


def plan_body(blocks, lists, ports, me_ref, table, orders):
    me = me_ref[0]
    far_count = 2 * blocks
    steps = blocks * K_SEL
    partner = me + 1 - 2 * (me % NC)
    for group_index, group in enumerate((me, partner)):

        def body(step, count):
            block, item = step // K_SEL, step % K_SEL
            entry = lists[item, group * blocks + block]
            place = entry - group * blocks
            far = (place < 0) | (place >= blocks)
            count = jnp.where(item == 0, 0, count)
            number = jnp.minimum(2 * block + count, far_count - 1)
            distance, index = route(me, entry, ports[entry], blocks)
            kind = jnp.where(index < 8, 0, 4) + jnp.where(
                distance == 0, 0, jnp.where(distance == 3, 1, jnp.where(distance == 1, 2, 3))
            )
            first = number
            for earlier in range(steps):
                same = (earlier < step) & (lists[earlier % K_SEL, group * blocks + earlier // K_SEL] == entry)
                first = jnp.where(same, jnp.minimum(first, orders[earlier]), first)
            orders[step] = number

            @pl.when(far)
            def _():
                table[group_index * far_count + number] = kind * 16 + index % 8
                table[(2 + group_index) * far_count + number] = jnp.where(first == number, 1, 0)

            if group_index == 0:
                table[4 * far_count + step] = jnp.where(far, blocks + first, place)
                table[4 * far_count + steps + step] = jnp.where(far, number, -1)
            return count + jnp.where(far, 1, 0)

        for step in range(steps):
            orders[step] = far_count
        lax.fori_loop(0, steps, body, jnp.int32(0))


def pick_body(far_count, table, *refs):
    gathered, out, sems = refs[:-2], refs[-2], refs[-1]
    for number in range(far_count):
        fetch(gathered, table[far_count + number], out.at[number], sems.at[number])
    for number in range(far_count):
        pltpu.make_async_copy(gathered[0].at[0], out.at[number], sems.at[number]).wait()


def attend_body(blocks, heads, scale, table, me_ref, query, key, value, grad, swapped, *refs):
    gathered, refs = refs[:8], refs[8:]
    attention, query_grad, near, mine, other, rows_of, totals, sems = refs
    me = me_ref[0]
    core = me % NC
    width = heads * HD
    far_count = 2 * blocks
    steps = blocks * K_SEL

    def start(step, carry):
        block, item = step // K_SEL, step % K_SEL
        slot = table[4 * far_count + step]
        number = table[4 * far_count + steps + step]
        rows = pl.ds(pl.multiple_of(item * BLK, BLK), BLK)

        @pl.when(number < 0)
        def _():
            source = pl.ds(pl.multiple_of(slot * BLK, BLK), BLK)
            pltpu.make_async_copy(key.at[source], rows_of.at[0, block, rows], sems.at[block, item, 0]).start()
            pltpu.make_async_copy(value.at[source], rows_of.at[1, block, rows], sems.at[block, item, 1]).start()

        @pl.when(number >= 0)
        def _():
            fetch(gathered, table[jnp.maximum(number, 0)], rows_of.at[core, block, rows], sems.at[block, item, core])
            pltpu.make_async_copy(
                swapped.at[jnp.maximum(number, 0)], rows_of.at[1 - core, block, rows], sems.at[block, item, 1 - core]
            ).start()

        return carry

    lax.fori_loop(0, steps, start, 0)

    @pl.loop(0, blocks + far_count)
    def _(slot):
        totals[0, slot] = jnp.zeros((BLK, width), jnp.float32)
        totals[1, slot] = jnp.zeros((BLK, width), jnp.float32)

    @pl.loop(0, blocks)
    def _(block):
        for item in range(K_SEL):
            rows = pl.ds(item * BLK, BLK)
            for kind in range(2):
                pltpu.make_async_copy(
                    key.at[pl.ds(0, BLK)], rows_of.at[kind, block, rows], sems.at[block, item, kind]
                ).wait()
        own_rows = pl.ds(pl.multiple_of(block * BLK, BLK), BLK)
        for head in range(heads):
            columns = pl.ds(head * HD, HD)
            q = query[own_rows, columns]
            g = grad[own_rows, columns]
            k = rows_of[0, block, :, columns]
            v = rows_of[1, block, :, columns]
            scores = lax.dot_general(q, k, (((1,), (1,)), ((), ())), preferred_element_type=jnp.float32) * scale
            top = jnp.max(scores, axis=-1, keepdims=True)
            raised = jnp.exp(scores - top)
            probs = raised * (1.0 / jnp.sum(raised, axis=-1, keepdims=True))
            probs_low = probs.astype(jnp.bfloat16)
            mixed = jnp.dot(probs_low, v, preferred_element_type=jnp.float32).astype(jnp.bfloat16)
            attention[own_rows, columns] = mixed
            delta = jnp.sum(g.astype(jnp.float32) * mixed.astype(jnp.float32), axis=-1, keepdims=True)
            grad_prob = lax.dot_general(g, v, (((1,), (1,)), ((), ())), preferred_element_type=jnp.float32)
            grad_score = (probs * (grad_prob - delta)).astype(jnp.bfloat16)
            query_grad[own_rows, columns] = (
                jnp.dot(grad_score, k, preferred_element_type=jnp.float32) * scale
            ).astype(jnp.bfloat16)
            key_terms = lax.dot_general(
                grad_score, q, (((0,), (0,)), ((), ())), preferred_element_type=jnp.float32
            ) * scale
            value_terms = lax.dot_general(
                probs_low, g, (((0,), (0,)), ((), ())), preferred_element_type=jnp.float32
            )
            for item in range(K_SEL):
                slot = table[4 * far_count + block * K_SEL + item]
                part = slice(item * BLK, (item + 1) * BLK)
                totals[0, slot, :, columns] += key_terms[part]
                totals[1, slot, :, columns] += value_terms[part]

    mine[...] = totals[core, blocks:].astype(jnp.bfloat16)
    other[...] = totals[1 - core, blocks:].astype(jnp.bfloat16)
    near[...] = totals[:, :blocks].reshape(2, blocks * BLK, width)


def add_terms(table, mine, theirs, cases):
    far_count = mine.shape[0]
    for group, terms in enumerate((mine, theirs)):

        def body(number, carry):
            code = table[group * far_count + number]
            first = table[(2 + group) * far_count + number] != 0
            for kind, ref in cases:

                @pl.when(first & (code // 16 == kind))
                def _():
                    index = code % 16

                    @pl.loop(0, 4)
                    def _(part):
                        rows = pl.ds(pl.multiple_of(part * (BLK // 4), BLK // 4), BLK // 4)
                        ref[index, rows] = (
                            ref[index, rows].astype(jnp.float32) + terms[number, rows].astype(jnp.float32)
                        ).astype(ref.dtype)

            return carry

        lax.fori_loop(0, far_count, body, 0)


def early_body(table, mine, theirs, far_low, far_high, up, down):
    @pl.loop(0, 8)
    def _(index):
        for ref in (far_low, far_high, up, down):
            ref[index] = jnp.zeros(ref.shape[1:], ref.dtype)

    add_terms(table, mine, theirs, ((3, far_low), (7, far_high), (6, up), (1, down)))


def late_body(table, mine, theirs, from_low, from_high, up, down):
    @pl.loop(0, 8)
    def _(index):
        up[index] = from_low[index]
        down[index] = from_high[index]

    add_terms(table, mine, theirs, ((2, up), (5, down)))


def mid_body(table, mine, theirs, low_first, high_first, low_second, high_second, own, down, up, far_low, far_high, first, second):
    f32, bf16 = jnp.float32, jnp.bfloat16

    @pl.loop(0, 8)
    def _(index):
        first[index] = low_first[index].astype(f32) + high_first[index].astype(f32)
        second[index] = low_second[index].astype(f32) + high_second[index].astype(f32)

    add_terms(table, mine, theirs, ((0, first), (4, second)))

    @pl.loop(0, 4)
    def _(index):
        own[index] = first[index].astype(bf16)
        down[index] = first[index + 4].astype(bf16)
        up[index] = second[index].astype(bf16)

    for index in range(2):
        far_low[index] = second[index + 4].astype(bf16)
        far_high[index] = second[index + 6].astype(bf16)


def turn_body(down, up, from_low, from_high, down_out, up_out):
    f32 = jnp.float32
    up_out[:2] = (up[:2].astype(f32) + from_low[...].astype(f32)).astype(jnp.bfloat16)
    up_out[2:] = up[2:]
    down_out[:2] = down[:2]
    down_out[2:] = (down[2:].astype(f32) + from_high[...].astype(f32)).astype(jnp.bfloat16)


def sum_body(own, from_low, from_high, mine, other):
    f32 = jnp.float32
    total = (own[...].astype(f32) + from_low[...].astype(f32) + from_high[...].astype(f32)).astype(jnp.bfloat16)
    mine[...] = total[:2]
    other[...] = total[2:]


def collect_body(blocks, ports, named, me_ref, near, mine, swapped, key_grad, value_grad):
    me = me_ref[0]
    core = me % NC
    f32 = jnp.float32

    @pl.loop(0, blocks)
    def _(block):
        rows = pl.ds(pl.multiple_of(block * BLK, BLK), BLK)
        port = ports[me * blocks + block]
        weight = named[me * blocks + block] != 0
        for kind, out in enumerate((key_grad, value_grad)):
            term = jnp.where(core == kind, mine[port].astype(f32), swapped[port].astype(f32))
            out[rows] = (near[kind, rows] + jnp.where(weight, term, 0.0)).astype(jnp.bfloat16)


def grad_terms(size, me, weight, rows, pieces):
    total = None
    for step, piece in pieces:
        width = piece.shape[1]
        start = lax.rem(me + step, size) * width
        term = lax.dot_general(
            piece[rows], weight[:, pl.ds(pl.multiple_of(start, HD), width)],
            (((1,), (1,)), ((), ())), preferred_element_type=jnp.float32,
        )
        total = term if total is None else total + term
    return total


def grad_body(size, steps, me_ref, weight, *refs):
    pieces, out = refs[:-1], refs[-1]
    me = me_ref[0]

    @pl.loop(0, out.shape[0] // BLK)
    def _(block):
        rows = pl.ds(pl.multiple_of(block * BLK, BLK), BLK)
        out[rows] = grad_terms(size, me, weight, rows, tuple(zip(steps, pieces)))


def grad_end_body(size, me_ref, weight, begun, low, high, out):
    me = me_ref[0]
    cut = low.shape[0]
    every = slice(None)
    for start, piece in ((0, low), (cut, high)):
        rows = slice(start, start + cut)
        out[rows] = (begun[rows] + grad_terms(size, me, weight, every, ((size // 2, piece),))).astype(jnp.bfloat16)


def project_body(size, me_ref, attention, weight, *outs):
    me = me_ref[0]
    width = attention.shape[1]

    @pl.loop(0, attention.shape[0] // BLK)
    def _(block):
        rows = pl.ds(pl.multiple_of(block * BLK, BLK), BLK)
        for step, out in enumerate(outs):
            start = lax.rem(me + step, size) * width
            out[rows] = jnp.dot(
                attention[rows], weight[:, pl.ds(pl.multiple_of(start, HD), width)],
                preferred_element_type=jnp.float32,
            ).astype(jnp.bfloat16)


def add(*terms):
    total = terms[0].astype(jnp.float32)
    for term in terms[1:]:
        total = total + term.astype(jnp.float32)
    return total.astype(jnp.bfloat16)


def ring_pair(pair):
    size = lax.axis_size("head")
    out = []
    for x, sign in ((pair[0], 1), (pair[1], -1)):
        out.append(lax.ppermute(x, "head", [(i, (i + sign) % size) for i in range(size)]))
    return tuple(out)


def layer(queries, key_states, value_states, block_lists, out_weight, out_grad):
    size = lax.axis_size("head")
    cells, width = queries.shape
    blocks = cells // BLK
    heads = width // HD
    me = lax.axis_index("seq").reshape(1).astype(jnp.int32)
    column = lax.axis_index("head").reshape(1).astype(jnp.int32)
    bf16, f32 = jnp.bfloat16, jnp.float32
    far = 2 * blocks

    def shape(*dims, dtype=bf16):
        return jax.ShapeDtypeStruct(dims, dtype)

    def call(body, in_specs, out_shape, *operands, out_specs=None, mib=10, scratch=()):
        return pl.pallas_call(
            body,
            in_specs=in_specs,
            out_specs=out_specs or [VMEM] * len(out_shape),
            out_shape=out_shape,
            scratch_shapes=scratch,
            compiler_params=pltpu.CompilerParams(vmem_limit_bytes=mib * 1024 * 1024),
        )(*operands)

    lists = block_lists.T
    piece = shape(2, BLK, width)
    mine, other = call(
        lambda *refs: pack_body(blocks, *refs), [VMEM, SMEM, ANY, ANY], [piece, piece],
        lists, me, key_states, value_states, scratch=[pltpu.SemaphoreType.DMA((2, 2))], mib=60,
    )
    entries = block_lists.reshape(-1)
    entry_group = jnp.arange(entries.shape[0], dtype=jnp.int32) // (blocks * K_SEL)
    far_entry = jnp.where(entries // blocks != entry_group, entries, -1)
    all_blocks = jnp.arange(block_lists.shape[0], dtype=jnp.int32)
    named = jnp.any(far_entry[None, :] == all_blocks[:, None], axis=1).astype(jnp.int32)
    ahead = jnp.concatenate([jnp.zeros((1,), jnp.int32), named[:-1]])
    ahead2 = jnp.concatenate([jnp.zeros((2,), jnp.int32), named[:-2]])
    inner = all_blocks % blocks
    ports = jnp.where(inner == 0, 0, jnp.where(inner == 1, ahead, jnp.maximum(ahead, ahead2)))

    (table,) = call(
        lambda *refs: plan_body(blocks, *refs), [SMEM] * 3,
        [shape(4 * far + 2 * blocks * K_SEL, dtype=jnp.int32)], lists, ports, me,
        out_specs=[SMEM], scratch=[pltpu.SMEM((blocks * K_SEL,), jnp.int32)],
    )

    half = size // 2
    cut = cells // 2
    ring = [(out_grad, out_grad)]
    for _ in range(1, half):
        ring.append(ring_pair(ring[-1]))
    across = ring_pair((ring[-1][0][:cut], ring[-1][1][cut:]))
    steps = [0]
    pieces = [out_grad]
    for step in range(1, half):
        steps += [size - step, step]
        pieces += ring[step]

    def join(*parts):
        total = sum(part.shape[0] for part in parts)
        return call(join_body, [VMEM] * len(parts), [shape(total, BLK, width)], *parts)[0]

    base = join(mine, swap(other))
    left, right = hop(base, 0, 1), hop(base, 0, -1)
    mid_a = join(base, left)
    low_a, high_a = hop(mid_a, 1, 1), hop(mid_a, 1, -1)
    mid_b = join(right, hop(left[:2], 0, 1), hop(right[2:], 0, -1))
    low_b, high_b = hop(mid_b, 1, 1), hop(mid_b, 1, -1)
    far_a, far_b = hop(low_a, 1, 1), hop(high_b, 1, -1)
    gathered = (mid_a, low_a, high_a, far_a, mid_b, low_b, high_b, far_b)
    (picked,) = call(
        lambda *refs: pick_body(far, *refs), [SMEM] + [ANY] * 8, [shape(far, BLK, width)],
        table, *gathered, scratch=[pltpu.SemaphoreType.DMA((far,))],
    )
    swapped = swap(picked)
    (begun,) = call(
        lambda *refs: grad_body(size, steps, *refs), [SMEM] + [VMEM] * size,
        [shape(cells, width, dtype=f32)], column, out_weight, *pieces,
    )
    (grad_attn,) = call(
        lambda *refs: grad_end_body(size, *refs), [SMEM] + [VMEM] * 4, [shape(cells, width)],
        column, out_weight, begun, *across,
    )
    attention, query_grad, near, terms, terms_other = call(
        lambda *refs: attend_body(blocks, heads, 1.0 / math.sqrt(HD), *refs),
        [SMEM, SMEM, VMEM, ANY, ANY, VMEM] + [ANY] * 9,
        [
            shape(cells, width), shape(cells, width), shape(2, cells, width, dtype=f32),
            shape(far, BLK, width), shape(far, BLK, width),
        ],
        table, me, queries, key_states, value_states, grad_attn, swapped, *gathered,
        scratch=[
            pltpu.VMEM((2, blocks, K_SEL * BLK, width), bf16),
            pltpu.VMEM((2, blocks + far, BLK, width), f32),
            pltpu.SemaphoreType.DMA((blocks, K_SEL, 2)),
        ],
        mib=16,
    )
    theirs = swap(terms_other)
    parts = call(
        lambda *refs: project_body(size, *refs), [SMEM, VMEM, VMEM], [shape(cells, width)] * size,
        column, attention, out_weight,
    )
    lead = (table, terms, theirs)
    lead_specs = [SMEM, VMEM, VMEM]
    eight = shape(8, BLK, width)
    far_low, far_high, up_b, down_a = call(early_body, lead_specs, [eight] * 4, *lead)
    from_low, from_high = hop(far_low, 1, 1), hop(far_high, 1, -1)
    low_b, high_a = hop(up_b, 1, 1), hop(down_a, 1, -1)
    ahead, back = ring_pair((parts[half][:cut], parts[half][cut:]))
    up_a, down_b = call(late_body, lead_specs + [VMEM] * 2, [eight] * 2, *lead, from_low, from_high)
    low_a, high_b = hop(up_a, 1, 1), hop(down_b, 1, -1)
    ahead = jnp.concatenate([add(parts[half - 1][:cut], ahead), parts[half - 1][cut:]])
    back = jnp.concatenate([parts[half + 1][:cut], add(parts[half + 1][cut:], back)])
    for distance in range(half - 2, -1, -1):
        ahead, back = ring_pair((ahead, back))
        if distance:
            ahead, back = add(parts[distance], ahead), add(parts[size - distance], back)
    attended = add(parts[0], ahead, back)
    own, down, up, far_low, far_high = call(
        mid_body, lead_specs + [VMEM] * 4, [shape(4, BLK, width)] * 3 + [piece] * 2,
        *lead, low_a, high_a, low_b, high_b,
        scratch=[pltpu.VMEM((8, BLK, width), f32)] * 2,
    )
    down, up = call(
        turn_body, [VMEM] * 4, [shape(4, BLK, width)] * 2,
        down, up, hop(far_low, 0, 1), hop(far_high, 0, -1),
    )
    mine, other = call(sum_body, [VMEM] * 3, [piece, piece], own, hop(up, 0, 1), hop(down, 0, -1))
    key_grad, value_grad = call(
        lambda *refs: collect_body(blocks, *refs), [SMEM, SMEM, SMEM] + [VMEM] * 3,
        [shape(cells, width)] * 2,
        ports, named, me, near, mine, swap(other),
    )
    return attended, query_grad, key_grad, value_grad


def solution(mesh):
    in_specs = (
        P("seq", "head"),
        P("seq", "head"),
        P("seq", "head"),
        P(),
        P("head", None),
        P("seq", "head"),
    )
    out_specs = (P("seq", "head"), P("seq", "head"), P("seq", "head"), P("seq", "head"))
    return jax.shard_map(layer, mesh=mesh, in_specs=in_specs, out_specs=out_specs, check_vma=False)
```

```python
import math

import jax
import jax.numpy as jnp
from jax import lax
from jax.experimental import pallas as pl
from jax.experimental.pallas import tpu as pltpu
from jax.sharding import PartitionSpec as P


HD = 128
BLK = 128
K_SEL = 4


SMEM = pl.BlockSpec(memory_space=pltpu.SMEM)
VMEM = pl.BlockSpec(memory_space=pltpu.VMEM)
ANY = pl.BlockSpec(memory_space=pl.ANY)
HBM = pl.BlockSpec(memory_space=pltpu.HBM)


NX, NY, NC = 4, 4, 2


def place_of(group):
    return group // (NY * NC), (group // NC) % NY, group % NC


def steps_of(leg, sign):
    pairs = []
    for group in range(NX * NY * NC):
        x, y, core = place_of(group)
        if (core == 0) == (leg == 0):
            x = (x + sign) % NX
        else:
            y = (y + sign) % NY
        pairs.append((group, (x * NY + y) * NC + core))
    return pairs


def swap_of():
    return [(group, group ^ 1) for group in range(NX * NY * NC)]


def hop(x, leg, sign):
    return lax.ppermute(x, "seq", steps_of(leg, sign))


def swap(x):
    return lax.ppermute(x, "seq", swap_of())


def route(me, entry, port, blocks):
    x, y, core = place_of(me)
    owner_x, owner_y, owner_core = place_of(entry // blocks)
    dx = (owner_x - x + NX) % NX
    dy = (owner_y - y + NY) % NY
    first = jnp.where(core == 0, dx, dy)
    second = jnp.where(core == 0, dy, dx)
    order = jnp.where(first == 0, 0, jnp.where(first == 3, 1, jnp.where(first == 1, 2, 3)))
    return second, order * 4 + 2 * jnp.where(owner_core == core, 0, 1) + port


def fetch(gathered, code, target, sem):
    for kind, source in enumerate(gathered):

        @pl.when(code // 16 == kind)
        def _():
            pltpu.make_async_copy(source.at[code % 16], target, sem).start()


def join_body(*refs):
    out, start = refs[-1], 0
    for ref in refs[:-1]:
        out[start:start + ref.shape[0]] = ref[...]
        start += ref.shape[0]


def pack_body(blocks, lists, me_ref, key, value, mine, other, sems):
    me = me_ref[0]
    core = me % NC
    row = lax.broadcasted_iota(jnp.int32, lists.shape, 1) - me * blocks
    entry = jnp.where((row < 0) | (row >= blocks), lists[...] - me * blocks, -1)
    named = [jnp.max(jnp.where(entry == block, 1.0, 0.0)) > 0.5 for block in range(blocks)]
    first = jnp.where(named[0], 0, jnp.where(named[1], 1, 2))
    second = jnp.where(named[2], 2, jnp.where(named[1], 1, 0))
    for port, block in enumerate((first, second)):
        rows = pl.ds(pl.multiple_of(block * BLK, BLK), BLK)

        @pl.when(core == 0)
        def _():
            pltpu.make_async_copy(key.at[rows], mine.at[port], sems.at[port, 0]).start()
            pltpu.make_async_copy(value.at[rows], other.at[port], sems.at[port, 1]).start()

        @pl.when(core != 0)
        def _():
            pltpu.make_async_copy(value.at[rows], mine.at[port], sems.at[port, 0]).start()
            pltpu.make_async_copy(key.at[rows], other.at[port], sems.at[port, 1]).start()

    for port in range(2):
        rows = pl.ds(0, BLK)
        pltpu.make_async_copy(key.at[rows], mine.at[port], sems.at[port, 0]).wait()
        pltpu.make_async_copy(key.at[rows], other.at[port], sems.at[port, 1]).wait()


def plan_body(blocks, lists, ports, me_ref, table):
    me = me_ref[0]
    far_count = 2 * blocks
    steps = blocks * K_SEL
    spare = table.shape[0] - 1
    partner = me + 1 - 2 * (me % NC)
    for group_index, group in enumerate((me, partner)):
        seen = []
        for block in range(blocks):
            count = jnp.int32(2 * block)
            row = []
            for item in range(K_SEL):
                step = block * K_SEL + item
                entry = lists[item, group * blocks + block]
                place = entry - group * blocks
                far = (place < 0) | (place >= blocks)
                number = count
                distance, index = route(me, entry, ports[entry], blocks)
                kind = jnp.where(index < 8, 0, 4) + jnp.where(
                    distance == 0, 0, jnp.where(distance == 3, 1, jnp.where(distance == 1, 2, 3))
                )
                first = number
                for earlier_entry, earlier_number in reversed(seen):
                    first = jnp.where(earlier_entry == entry, earlier_number, first)
                row.append((entry, number))
                table[jnp.where(far, group_index * far_count + number, spare)] = kind * 16 + index % 8
                table[jnp.where(far, (2 + group_index) * far_count + number, spare)] = jnp.where(first == number, 1, 0)
                if group_index == 0:
                    table[4 * far_count + step] = jnp.where(far, blocks + first, place)
                    table[4 * far_count + steps + step] = jnp.where(far, number, -1)
                count = count + jnp.where(far, 1, 0)
            seen += row


def pick_body(far_count, table, *refs):
    gathered, out, sems = refs[:-2], refs[-2], refs[-1]
    for number in range(far_count):
        fetch(gathered, table[far_count + number], out.at[number], sems.at[number])
    for number in range(far_count):
        pltpu.make_async_copy(gathered[0].at[0], out.at[number], sems.at[number]).wait()


def attend_body(blocks, heads, scale, table, me_ref, query, key, value, grad, swapped, *refs):
    gathered, refs = refs[:8], refs[8:]
    attention, query_grad, near, mine, other, rows_of, totals, sems = refs
    me = me_ref[0]
    core = me % NC
    width = heads * HD
    far_count = 2 * blocks
    steps = blocks * K_SEL

    def start(step, carry):
        block, item = step // K_SEL, step % K_SEL
        slot = table[4 * far_count + step]
        number = table[4 * far_count + steps + step]
        rows = pl.ds(pl.multiple_of(item * BLK, BLK), BLK)

        @pl.when(number < 0)
        def _():
            source = pl.ds(pl.multiple_of(slot * BLK, BLK), BLK)
            pltpu.make_async_copy(key.at[source], rows_of.at[0, block, rows], sems.at[block, item, 0]).start()
            pltpu.make_async_copy(value.at[source], rows_of.at[1, block, rows], sems.at[block, item, 1]).start()

        @pl.when(number >= 0)
        def _():
            fetch(gathered, table[jnp.maximum(number, 0)], rows_of.at[core, block, rows], sems.at[block, item, core])
            pltpu.make_async_copy(
                swapped.at[jnp.maximum(number, 0)], rows_of.at[1 - core, block, rows], sems.at[block, item, 1 - core]
            ).start()

        return carry

    lax.fori_loop(0, steps, start, 0)

    @pl.loop(0, blocks + far_count)
    def _(slot):
        totals[0, slot] = jnp.zeros((BLK, width), jnp.float32)
        totals[1, slot] = jnp.zeros((BLK, width), jnp.float32)

    @pl.loop(0, blocks)
    def _(block):
        for item in range(K_SEL):
            rows = pl.ds(item * BLK, BLK)
            for kind in range(2):
                pltpu.make_async_copy(
                    key.at[pl.ds(0, BLK)], rows_of.at[kind, block, rows], sems.at[block, item, kind]
                ).wait()
        own_rows = pl.ds(pl.multiple_of(block * BLK, BLK), BLK)
        f32, bf16 = jnp.float32, jnp.bfloat16
        every = [pl.ds(head * HD, HD) for head in range(heads)]

        def rows_times_rows(left, right):
            return lax.dot_general(left, right, (((1,), (1,)), ((), ())), preferred_element_type=f32)

        def columns_times(left, right):
            return lax.dot_general(left, right, (((0,), (0,)), ((), ())), preferred_element_type=f32)

        qs = [query[own_rows, columns] for columns in every]
        gs = [grad[own_rows, columns] for columns in every]
        ks = [rows_of[0, block, :, columns] for columns in every]
        vs = [rows_of[1, block, :, columns] for columns in every]
        scores = [rows_times_rows(q, k) * scale for q, k in zip(qs, ks)]
        grad_probs = [rows_times_rows(g, v) for g, v in zip(gs, vs)]
        raised = [jnp.exp(x - jnp.max(x, axis=-1, keepdims=True)) for x in scores]
        probs = [x * (1.0 / jnp.sum(x, axis=-1, keepdims=True)) for x in raised]
        lows = [x.astype(bf16) for x in probs]
        mixed = [jnp.dot(low, v, preferred_element_type=f32).astype(bf16) for low, v in zip(lows, vs)]
        deltas = [jnp.sum(g.astype(f32) * x.astype(f32), axis=-1, keepdims=True) for g, x in zip(gs, mixed)]
        grad_scores = [(p * (x - d)).astype(bf16) for p, x, d in zip(probs, grad_probs, deltas)]
        for head, columns in enumerate(every):
            attention[own_rows, columns] = mixed[head]
            query_grad[own_rows, columns] = (
                jnp.dot(grad_scores[head], ks[head], preferred_element_type=f32) * scale
            ).astype(bf16)
        for head, columns in enumerate(every):
            key_terms = columns_times(grad_scores[head], qs[head]) * scale
            value_terms = columns_times(lows[head], gs[head])
            for item in range(K_SEL):
                slot = table[4 * far_count + block * K_SEL + item]
                part = slice(item * BLK, (item + 1) * BLK)
                totals[0, slot, :, columns] += key_terms[part]
                totals[1, slot, :, columns] += value_terms[part]

    @pl.loop(0, far_count)
    def _(number):
        mine[number] = totals[core, blocks + number].astype(jnp.bfloat16)
        other[number] = totals[1 - core, blocks + number].astype(jnp.bfloat16)

    @pl.loop(0, blocks)
    def _(block):
        rows = pl.ds(pl.multiple_of(block * BLK, BLK), BLK)
        near[0, rows] = totals[0, block]
        near[1, rows] = totals[1, block]


def add_terms(table, mine, theirs, cases):
    far_count = mine.shape[0]
    for group, terms in enumerate((mine, theirs)):

        def body(number, carry):
            code = table[group * far_count + number]
            first = table[(2 + group) * far_count + number] != 0
            for kind, ref in cases:

                @pl.when(first & (code // 16 == kind))
                def _():
                    index = code % 16

                    @pl.loop(0, 4)
                    def _(part):
                        rows = pl.ds(pl.multiple_of(part * (BLK // 4), BLK // 4), BLK // 4)
                        ref[index, rows] = (
                            ref[index, rows].astype(jnp.float32) + terms[number, rows].astype(jnp.float32)
                        ).astype(ref.dtype)

            return carry

        lax.fori_loop(0, far_count, body, 0)


def early_body(table, mine, theirs, far_low, far_high, up, down):
    @pl.loop(0, 8)
    def _(index):
        for ref in (far_low, far_high, up, down):
            ref[index] = jnp.zeros(ref.shape[1:], ref.dtype)

    add_terms(table, mine, theirs, ((3, far_low), (7, far_high), (6, up), (1, down)))


def late_body(table, mine, theirs, from_low, from_high, up, down):
    @pl.loop(0, 8)
    def _(index):
        up[index] = from_low[index]
        down[index] = from_high[index]

    add_terms(table, mine, theirs, ((2, up), (5, down)))


def mid_body(table, mine, theirs, low_first, high_first, low_second, high_second, own, down, up, far_low, far_high, first, second):
    f32, bf16 = jnp.float32, jnp.bfloat16

    @pl.loop(0, 8)
    def _(index):
        first[index] = low_first[index].astype(f32) + high_first[index].astype(f32)
        second[index] = low_second[index].astype(f32) + high_second[index].astype(f32)

    add_terms(table, mine, theirs, ((0, first), (4, second)))

    @pl.loop(0, 4)
    def _(index):
        own[index] = first[index].astype(bf16)
        down[index] = first[index + 4].astype(bf16)
        up[index] = second[index].astype(bf16)

    for index in range(2):
        far_low[index] = second[index + 4].astype(bf16)
        far_high[index] = second[index + 6].astype(bf16)


def turn_body(down, up, from_low, from_high, down_out, up_out):
    f32 = jnp.float32
    up_out[:2] = (up[:2].astype(f32) + from_low[...].astype(f32)).astype(jnp.bfloat16)
    up_out[2:] = up[2:]
    down_out[:2] = down[:2]
    down_out[2:] = (down[2:].astype(f32) + from_high[...].astype(f32)).astype(jnp.bfloat16)


def sum_body(own, from_low, from_high, mine, other):
    f32 = jnp.float32
    total = (own[...].astype(f32) + from_low[...].astype(f32) + from_high[...].astype(f32)).astype(jnp.bfloat16)
    mine[...] = total[:2]
    other[...] = total[2:]


def collect_body(blocks, ports, named, me_ref, near, mine, swapped, key_grad, value_grad):
    me = me_ref[0]
    core = me % NC
    f32 = jnp.float32

    @pl.loop(0, blocks)
    def _(block):
        rows = pl.ds(pl.multiple_of(block * BLK, BLK), BLK)
        port = ports[me * blocks + block]
        weight = named[me * blocks + block] != 0
        for kind, out in enumerate((key_grad, value_grad)):
            term = jnp.where(core == kind, mine[port].astype(f32), swapped[port].astype(f32))
            out[rows] = (near[kind, rows] + jnp.where(weight, term, 0.0)).astype(jnp.bfloat16)


def grad_body(size, me_ref, weight, *refs):
    pieces, (out, held, sems) = refs[:-3], refs[-3:]
    me = me_ref[0]
    width = out.shape[1]
    for number, piece in enumerate(pieces):
        pltpu.make_async_copy(piece, held.at[number], sems.at[number]).start()
    out[...] = jnp.zeros_like(out)

    @pl.loop(0, len(pieces))
    def _(number):
        pltpu.make_async_copy(pieces[0], held.at[number], sems.at[number]).wait()
        half = (number + 1) // 2
        step = jnp.where(number % 2 == 1, size - half, half)
        start = lax.rem(me + step, size) * width
        out[...] += lax.dot_general(
            held[number], weight[:, pl.ds(pl.multiple_of(start, HD), width)],
            (((1,), (1,)), ((), ())), preferred_element_type=jnp.float32,
        )


def half_body(low, high, low_out, high_out, sems):
    cut = low_out.shape[0]
    copies = (
        pltpu.make_async_copy(low.at[pl.ds(0, cut)], low_out, sems.at[0]),
        pltpu.make_async_copy(high.at[pl.ds(cut, cut)], high_out, sems.at[1]),
    )
    for copy in copies:
        copy.start()
    for copy in copies:
        copy.wait()


def grad_end_body(size, me_ref, weight, begun, from_low, from_high, low, high, out):
    me = me_ref[0]
    half = size // 2
    cut, width = low.shape

    def term(piece, step):
        start = lax.rem(me + step, size) * width
        return lax.dot_general(
            piece, weight[:, pl.ds(pl.multiple_of(start, HD), width)],
            (((1,), (1,)), ((), ())), preferred_element_type=jnp.float32,
        )

    total = begun[...] + term(from_low[...], size - half + 1) + term(from_high[...], half - 1)
    for rows, piece in ((slice(0, cut), low), (slice(cut, 2 * cut), high)):
        out[rows] = (total[rows] + term(piece[...], half)).astype(jnp.bfloat16)


def project_body(size, me_ref, attention, weight, *outs):
    me = me_ref[0]
    width = attention.shape[1]

    @pl.loop(0, attention.shape[0] // BLK)
    def _(block):
        rows = pl.ds(pl.multiple_of(block * BLK, BLK), BLK)
        for step, out in enumerate(outs):
            start = lax.rem(me + step, size) * width
            out[rows] = jnp.dot(
                attention[rows], weight[:, pl.ds(pl.multiple_of(start, HD), width)],
                preferred_element_type=jnp.float32,
            ).astype(jnp.bfloat16)


def add(*terms):
    total = terms[0].astype(jnp.float32)
    for term in terms[1:]:
        total = total + term.astype(jnp.float32)
    return total.astype(jnp.bfloat16)


def ring_pair(pair):
    size = lax.axis_size("head")
    out = []
    for x, sign in ((pair[0], 1), (pair[1], -1)):
        out.append(lax.ppermute(x, "head", [(i, (i + sign) % size) for i in range(size)]))
    return tuple(out)


def layer(queries, key_states, value_states, block_lists, out_weight, out_grad):
    size = lax.axis_size("head")
    cells, width = queries.shape
    blocks = cells // BLK
    heads = width // HD
    me = lax.axis_index("seq").reshape(1).astype(jnp.int32)
    column = lax.axis_index("head").reshape(1).astype(jnp.int32)
    bf16, f32 = jnp.bfloat16, jnp.float32
    far = 2 * blocks

    def shape(*dims, dtype=bf16):
        return jax.ShapeDtypeStruct(dims, dtype)

    def call(body, in_specs, out_shape, *operands, out_specs=None, mib=10, scratch=()):
        return pl.pallas_call(
            body,
            in_specs=in_specs,
            out_specs=out_specs or [VMEM] * len(out_shape),
            out_shape=out_shape,
            scratch_shapes=scratch,
            compiler_params=pltpu.CompilerParams(vmem_limit_bytes=mib * 1024 * 1024),
        )(*operands)

    lists = block_lists.T
    piece = shape(2, BLK, width)
    mine, other = call(
        lambda *refs: pack_body(blocks, *refs), [VMEM, SMEM, HBM, HBM], [piece, piece],
        lists, me,
        *(pltpu.with_memory_space_constraint(x, pltpu.HBM) for x in (key_states, value_states)),
        scratch=[pltpu.SemaphoreType.DMA((2, 2))],
    )
    entries = block_lists.reshape(-1)
    entry_group = jnp.arange(entries.shape[0], dtype=jnp.int32) // (blocks * K_SEL)
    far_entry = jnp.where(entries // blocks != entry_group, entries, -1)
    all_blocks = jnp.arange(block_lists.shape[0], dtype=jnp.int32)
    named = jnp.any(far_entry[None, :] == all_blocks[:, None], axis=1).astype(jnp.int32)
    ahead = jnp.concatenate([jnp.zeros((1,), jnp.int32), named[:-1]])
    ahead2 = jnp.concatenate([jnp.zeros((2,), jnp.int32), named[:-2]])
    inner = all_blocks % blocks
    ports = jnp.where(inner == 0, 0, jnp.where(inner == 1, ahead, jnp.maximum(ahead, ahead2)))

    (table,) = call(
        lambda *refs: plan_body(blocks, *refs), [SMEM] * 3,
        [shape(4 * far + 2 * blocks * K_SEL + 1, dtype=jnp.int32)], lists, ports, me, out_specs=[SMEM],
    )

    half = size // 2
    cut = cells // 2
    ring = [(out_grad, out_grad)]
    for _ in range(1, half):
        ring.append(ring_pair(ring[-1]))
    across = ring_pair(call(
        half_body, [HBM] * 2, [shape(cut, width)] * 2, *ring[-1],
        scratch=[pltpu.SemaphoreType.DMA((2,))],
    ))
    pieces = [out_grad]
    for step in range(1, half - 1):
        pieces += ring[step]

    def join(*parts):
        total = sum(part.shape[0] for part in parts)
        return call(join_body, [VMEM] * len(parts), [shape(total, BLK, width)], *parts)[0]

    base = join(mine, swap(other))
    left, right = hop(base, 0, 1), hop(base, 0, -1)
    mid_a = join(base, left)
    low_a, high_a = hop(mid_a, 1, 1), hop(mid_a, 1, -1)
    mid_b = join(right, hop(left[:2], 0, 1), hop(right[2:], 0, -1))
    low_b, high_b = hop(mid_b, 1, 1), hop(mid_b, 1, -1)
    far_a, far_b = hop(low_a, 1, 1), hop(high_b, 1, -1)
    gathered = (mid_a, low_a, high_a, far_a, mid_b, low_b, high_b, far_b)
    (picked,) = call(
        lambda *refs: pick_body(far, *refs), [SMEM] + [ANY] * 8, [shape(far, BLK, width)],
        table, *gathered, scratch=[pltpu.SemaphoreType.DMA((far,))],
    )
    swapped = swap(picked)
    (begun,) = call(
        lambda *refs: grad_body(size, *refs), [SMEM, VMEM] + [HBM] * len(pieces),
        [shape(cells, width, dtype=f32)], column, out_weight, *pieces,
        scratch=[pltpu.VMEM((len(pieces), cells, width), bf16), pltpu.SemaphoreType.DMA((len(pieces),))],
    )
    (grad_attn,) = call(
        lambda *refs: grad_end_body(size, *refs), [SMEM] + [VMEM] * 6, [shape(cells, width)],
        column, out_weight, begun, *ring[-1], *across,
    )
    attention, query_grad, near, terms, terms_other = call(
        lambda *refs: attend_body(blocks, heads, 1.0 / math.sqrt(HD), *refs),
        [SMEM, SMEM, VMEM, ANY, ANY, VMEM] + [ANY] * 9,
        [
            shape(cells, width), shape(cells, width), shape(2, cells, width, dtype=f32),
            shape(far, BLK, width), shape(far, BLK, width),
        ],
        table, me, queries, key_states, value_states, grad_attn, swapped, *gathered,
        scratch=[
            pltpu.VMEM((2, blocks, K_SEL * BLK, width), bf16),
            pltpu.VMEM((2, blocks + far, BLK, width), f32),
            pltpu.SemaphoreType.DMA((blocks, K_SEL, 2)),
        ],
        mib=16,
    )
    theirs = swap(terms_other)
    parts = call(
        lambda *refs: project_body(size, *refs), [SMEM, VMEM, VMEM], [shape(cells, width)] * size,
        column, attention, out_weight,
    )
    lead = (table, terms, theirs)
    lead_specs = [SMEM, VMEM, VMEM]
    eight = shape(8, BLK, width)
    far_low, far_high, up_b, down_a = call(early_body, lead_specs, [eight] * 4, *lead)
    from_low, from_high = hop(far_low, 1, 1), hop(far_high, 1, -1)
    low_b, high_a = hop(up_b, 1, 1), hop(down_a, 1, -1)
    ahead, back = ring_pair((parts[half][:cut], parts[half][cut:]))
    up_a, down_b = call(late_body, lead_specs + [VMEM] * 2, [eight] * 2, *lead, from_low, from_high)
    low_a, high_b = hop(up_a, 1, 1), hop(down_b, 1, -1)
    ahead = jnp.concatenate([add(parts[half - 1][:cut], ahead), parts[half - 1][cut:]])
    back = jnp.concatenate([parts[half + 1][:cut], add(parts[half + 1][cut:], back)])
    for distance in range(half - 2, -1, -1):
        ahead, back = ring_pair((ahead, back))
        if distance:
            ahead, back = add(parts[distance], ahead), add(parts[size - distance], back)
    attended = add(parts[0], ahead, back)
    own, down, up, far_low, far_high = call(
        mid_body, lead_specs + [VMEM] * 4, [shape(4, BLK, width)] * 3 + [piece] * 2,
        *lead, low_a, high_a, low_b, high_b,
        scratch=[pltpu.VMEM((8, BLK, width), f32)] * 2,
    )
    down, up = call(
        turn_body, [VMEM] * 4, [shape(4, BLK, width)] * 2,
        down, up, hop(far_low, 0, 1), hop(far_high, 0, -1),
    )
    mine, other = call(sum_body, [VMEM] * 3, [piece, piece], own, hop(up, 0, 1), hop(down, 0, -1))
    key_grad, value_grad = call(
        lambda *refs: collect_body(blocks, *refs), [SMEM, SMEM, SMEM] + [VMEM] * 3,
        [shape(cells, width)] * 2,
        ports, named, me, near, mine, swap(other),
    )
    return attended, query_grad, key_grad, value_grad


def solution(mesh):
    in_specs = (
        P("seq", "head"),
        P("seq", "head"),
        P("seq", "head"),
        P(),
        P("head", None),
        P("seq", "head"),
    )
    out_specs = (P("seq", "head"), P("seq", "head"), P("seq", "head"), P("seq", "head"))
    return jax.shard_map(layer, mesh=mesh, in_specs=in_specs, out_specs=out_specs, check_vma=False)
```

```python
import math

import jax
import jax.numpy as jnp
from jax import lax
from jax.experimental import pallas as pl
from jax.experimental.pallas import tpu as pltpu
from jax.sharding import PartitionSpec as P


HD = 128
BLK = 128
K_SEL = 4


SMEM = pl.BlockSpec(memory_space=pltpu.SMEM)
VMEM = pl.BlockSpec(memory_space=pltpu.VMEM)
ANY = pl.BlockSpec(memory_space=pl.ANY)
HBM = pl.BlockSpec(memory_space=pltpu.HBM)


NX, NY, NC = 4, 4, 2


def place_of(group):
    return group // (NY * NC), (group // NC) % NY, group % NC


def steps_of(leg, sign):
    pairs = []
    for group in range(NX * NY * NC):
        x, y, core = place_of(group)
        if (core == 0) == (leg == 0):
            x = (x + sign) % NX
        else:
            y = (y + sign) % NY
        pairs.append((group, (x * NY + y) * NC + core))
    return pairs


def swap_of():
    return [(group, group ^ 1) for group in range(NX * NY * NC)]


def hop(x, leg, sign):
    return lax.ppermute(x, "seq", steps_of(leg, sign))


def swap(x):
    return lax.ppermute(x, "seq", swap_of())


def route(me, entry, port, blocks):
    x, y, core = place_of(me)
    owner_x, owner_y, owner_core = place_of(entry // blocks)
    dx = (owner_x - x + NX) % NX
    dy = (owner_y - y + NY) % NY
    first = jnp.where(core == 0, dx, dy)
    second = jnp.where(core == 0, dy, dx)
    order = jnp.where(first == 0, 0, jnp.where(first == 3, 1, jnp.where(first == 1, 2, 3)))
    return second, order * 4 + 2 * jnp.where(owner_core == core, 0, 1) + port


def fetch(gathered, code, target, sem):
    for kind, source in enumerate(gathered):

        @pl.when(code // 16 == kind)
        def _():
            pltpu.make_async_copy(source.at[code % 16], target, sem).start()


def join_body(*refs):
    out, start = refs[-1], 0
    for ref in refs[:-1]:
        out[start:start + ref.shape[0]] = ref[...]
        start += ref.shape[0]


def pack_body(blocks, lists, me_ref, key, value, mine, other, sems):
    me = me_ref[0]
    core = me % NC
    row = lax.broadcasted_iota(jnp.int32, lists.shape, 1) - me * blocks
    entry = jnp.where((row < 0) | (row >= blocks), lists[...] - me * blocks, -1)
    named = [jnp.max(jnp.where(entry == block, 1.0, 0.0)) > 0.5 for block in range(blocks)]
    first = jnp.where(named[0], 0, jnp.where(named[1], 1, 2))
    second = jnp.where(named[2], 2, jnp.where(named[1], 1, 0))
    for port, block in enumerate((first, second)):
        rows = pl.ds(pl.multiple_of(block * BLK, BLK), BLK)

        @pl.when(core == 0)
        def _():
            pltpu.make_async_copy(key.at[rows], mine.at[port], sems.at[port, 0]).start()
            pltpu.make_async_copy(value.at[rows], other.at[port], sems.at[port, 1]).start()

        @pl.when(core != 0)
        def _():
            pltpu.make_async_copy(value.at[rows], mine.at[port], sems.at[port, 0]).start()
            pltpu.make_async_copy(key.at[rows], other.at[port], sems.at[port, 1]).start()

    for port in range(2):
        rows = pl.ds(0, BLK)
        pltpu.make_async_copy(key.at[rows], mine.at[port], sems.at[port, 0]).wait()
        pltpu.make_async_copy(key.at[rows], other.at[port], sems.at[port, 1]).wait()


def plan_body(blocks, lists, ports, me_ref, table):
    me = me_ref[0]
    far_count = 2 * blocks
    steps = blocks * K_SEL
    spare = table.shape[0] - 1
    partner = me + 1 - 2 * (me % NC)
    for group_index, group in enumerate((me, partner)):
        seen = []
        for block in range(blocks):
            count = jnp.int32(2 * block)
            row = []
            for item in range(K_SEL):
                step = block * K_SEL + item
                entry = lists[item, group * blocks + block]
                place = entry - group * blocks
                far = (place < 0) | (place >= blocks)
                number = count
                distance, index = route(me, entry, ports[entry], blocks)
                kind = jnp.where(index < 8, 0, 4) + jnp.where(
                    distance == 0, 0, jnp.where(distance == 3, 1, jnp.where(distance == 1, 2, 3))
                )
                first = number
                for earlier_entry, earlier_number in reversed(seen):
                    first = jnp.where(earlier_entry == entry, earlier_number, first)
                row.append((entry, number))
                table[jnp.where(far, group_index * far_count + number, spare)] = kind * 16 + index % 8
                table[jnp.where(far, (2 + group_index) * far_count + number, spare)] = jnp.where(first == number, 1, 0)
                if group_index == 0:
                    table[4 * far_count + step] = jnp.where(far, blocks + first, place)
                    table[4 * far_count + steps + step] = jnp.where(far, number, -1)
                count = count + jnp.where(far, 1, 0)
            seen += row


def pick_body(far_count, table, *refs):
    gathered, out, sems = refs[:-2], refs[-2], refs[-1]
    for number in range(far_count):
        fetch(gathered, table[far_count + number], out.at[number], sems.at[number])
    for number in range(far_count):
        pltpu.make_async_copy(gathered[0].at[0], out.at[number], sems.at[number]).wait()


def attend_body(blocks, heads, scale, table, me_ref, query, key, value, grad, swapped, *refs):
    gathered, refs = refs[:8], refs[8:]
    attention, query_grad, near, mine, other, rows_of, totals, sems = refs
    me = me_ref[0]
    core = me % NC
    width = heads * HD
    far_count = 2 * blocks
    steps = blocks * K_SEL

    def start(step, carry):
        block, item = step // K_SEL, step % K_SEL
        slot = table[4 * far_count + step]
        number = table[4 * far_count + steps + step]
        rows = pl.ds(pl.multiple_of(item * BLK, BLK), BLK)

        @pl.when(number < 0)
        def _():
            source = pl.ds(pl.multiple_of(slot * BLK, BLK), BLK)
            pltpu.make_async_copy(key.at[source], rows_of.at[0, block, rows], sems.at[block, item, 0]).start()
            pltpu.make_async_copy(value.at[source], rows_of.at[1, block, rows], sems.at[block, item, 1]).start()

        @pl.when(number >= 0)
        def _():
            fetch(gathered, table[jnp.maximum(number, 0)], rows_of.at[core, block, rows], sems.at[block, item, core])
            pltpu.make_async_copy(
                swapped.at[jnp.maximum(number, 0)], rows_of.at[1 - core, block, rows], sems.at[block, item, 1 - core]
            ).start()

        return carry

    lax.fori_loop(0, steps, start, 0)

    @pl.loop(0, blocks + far_count)
    def _(slot):
        totals[0, slot] = jnp.zeros((BLK, width), jnp.float32)
        totals[1, slot] = jnp.zeros((BLK, width), jnp.float32)

    @pl.loop(0, blocks)
    def _(block):
        for item in range(K_SEL):
            rows = pl.ds(item * BLK, BLK)
            for kind in range(2):
                pltpu.make_async_copy(
                    key.at[pl.ds(0, BLK)], rows_of.at[kind, block, rows], sems.at[block, item, kind]
                ).wait()
        own_rows = pl.ds(pl.multiple_of(block * BLK, BLK), BLK)
        f32, bf16 = jnp.float32, jnp.bfloat16
        every = [pl.ds(head * HD, HD) for head in range(heads)]

        def rows_times_rows(left, right):
            return lax.dot_general(left, right, (((1,), (1,)), ((), ())), preferred_element_type=f32)

        def columns_times(left, right):
            return lax.dot_general(left, right, (((0,), (0,)), ((), ())), preferred_element_type=f32)

        qs = [query[own_rows, columns] for columns in every]
        gs = [grad[own_rows, columns] for columns in every]
        ks = [rows_of[0, block, :, columns] for columns in every]
        vs = [rows_of[1, block, :, columns] for columns in every]
        scores = [rows_times_rows(q, k) * scale for q, k in zip(qs, ks)]
        grad_probs = [rows_times_rows(g, v) for g, v in zip(gs, vs)]
        raised = [jnp.exp(x - jnp.max(x, axis=-1, keepdims=True)) for x in scores]
        probs = [x * (1.0 / jnp.sum(x, axis=-1, keepdims=True)) for x in raised]
        lows = [x.astype(bf16) for x in probs]
        mixed = [jnp.dot(low, v, preferred_element_type=f32).astype(bf16) for low, v in zip(lows, vs)]
        deltas = [jnp.sum(g.astype(f32) * x.astype(f32), axis=-1, keepdims=True) for g, x in zip(gs, mixed)]
        grad_scores = [(p * (x - d)).astype(bf16) for p, x, d in zip(probs, grad_probs, deltas)]
        for head, columns in enumerate(every):
            attention[own_rows, columns] = mixed[head]
            query_grad[own_rows, columns] = (
                jnp.dot(grad_scores[head], ks[head], preferred_element_type=f32) * scale
            ).astype(bf16)
        for head, columns in enumerate(every):
            key_terms = columns_times(grad_scores[head], qs[head]) * scale
            value_terms = columns_times(lows[head], gs[head])
            for item in range(K_SEL):
                slot = table[4 * far_count + block * K_SEL + item]
                part = slice(item * BLK, (item + 1) * BLK)
                totals[0, slot, :, columns] += key_terms[part]
                totals[1, slot, :, columns] += value_terms[part]

    @pl.loop(0, far_count)
    def _(number):
        mine[number] = totals[core, blocks + number].astype(jnp.bfloat16)
        other[number] = totals[1 - core, blocks + number].astype(jnp.bfloat16)

    @pl.loop(0, blocks)
    def _(block):
        rows = pl.ds(pl.multiple_of(block * BLK, BLK), BLK)
        near[0, rows] = totals[0, block]
        near[1, rows] = totals[1, block]


def add_terms(table, mine, theirs, cases):
    far_count = mine.shape[0]
    for group, terms in enumerate((mine, theirs)):

        def body(number, carry):
            code = table[group * far_count + number]
            first = table[(2 + group) * far_count + number] != 0
            for kind, low, high, ref in cases:

                @pl.when(first & (code >= kind * 16 + low) & (code < kind * 16 + high))
                def _():
                    index = code - (kind * 16 + low)

                    @pl.loop(0, 4)
                    def _(part):
                        rows = pl.ds(pl.multiple_of(part * (BLK // 4), BLK // 4), BLK // 4)
                        ref[index, rows] = (
                            ref[index, rows].astype(jnp.float32) + terms[number, rows].astype(jnp.float32)
                        ).astype(ref.dtype)

            return carry

        lax.fori_loop(0, far_count, body, 0)


def pair_body(first_kind, second_kind, table, mine, theirs, first, second):
    @pl.loop(0, 8)
    def _(index):
        for ref in (first, second):
            ref[index] = jnp.zeros(ref.shape[1:], ref.dtype)

    add_terms(table, mine, theirs, ((first_kind, 0, 8, first), (second_kind, 0, 8, second)))


def late_body(table, mine, theirs, from_low, from_high, up, down):
    @pl.loop(0, 8)
    def _(index):
        up[index] = from_low[index]
        down[index] = from_high[index]

    add_terms(table, mine, theirs, ((2, 0, 8, up), (5, 0, 8, down)))


def opposite_body(table, mine, theirs, low_second, high_second, far_low, far_high, total):
    f32, bf16 = jnp.float32, jnp.bfloat16

    @pl.loop(0, 4)
    def _(index):
        total[index] = low_second[index + 4].astype(f32) + high_second[index + 4].astype(f32)

    add_terms(table, mine, theirs, ((4, 4, 8, total),))
    for index in range(2):
        far_low[index] = total[index].astype(bf16)
        far_high[index] = total[index + 2].astype(bf16)


def mid_body(table, mine, theirs, low_first, high_first, low_second, high_second, own, down, up, first, second):
    f32, bf16 = jnp.float32, jnp.bfloat16

    @pl.loop(0, 4)
    def _(index):
        first[index] = low_first[index].astype(f32) + high_first[index].astype(f32)
        first[index + 4] = low_first[index + 4].astype(f32) + high_first[index + 4].astype(f32)
        second[index] = low_second[index].astype(f32) + high_second[index].astype(f32)

    add_terms(table, mine, theirs, ((0, 0, 8, first), (4, 0, 4, second)))

    @pl.loop(0, 4)
    def _(index):
        own[index] = first[index].astype(bf16)
        down[index] = first[index + 4].astype(bf16)
        up[index] = second[index].astype(bf16)


def turn_body(down, up, from_low, from_high, down_out, up_out):
    f32 = jnp.float32
    up_out[:2] = (up[:2].astype(f32) + from_low[...].astype(f32)).astype(jnp.bfloat16)
    up_out[2:] = up[2:]
    down_out[:2] = down[:2]
    down_out[2:] = (down[2:].astype(f32) + from_high[...].astype(f32)).astype(jnp.bfloat16)


def sum_body(own, from_low, from_high, mine, other):
    f32 = jnp.float32
    total = (own[...].astype(f32) + from_low[...].astype(f32) + from_high[...].astype(f32)).astype(jnp.bfloat16)
    mine[...] = total[:2]
    other[...] = total[2:]


def collect_body(blocks, ports, named, me_ref, near, mine, swapped, key_grad, value_grad):
    me = me_ref[0]
    core = me % NC
    f32 = jnp.float32

    @pl.loop(0, blocks)
    def _(block):
        rows = pl.ds(pl.multiple_of(block * BLK, BLK), BLK)
        port = ports[me * blocks + block]
        weight = named[me * blocks + block] != 0
        for kind, out in enumerate((key_grad, value_grad)):
            term = jnp.where(core == kind, mine[port].astype(f32), swapped[port].astype(f32))
            out[rows] = (near[kind, rows] + jnp.where(weight, term, 0.0)).astype(jnp.bfloat16)


def grad_body(size, me_ref, weight, *refs):
    pieces, (out, held, sems) = refs[:-3], refs[-3:]
    me = me_ref[0]
    width = out.shape[1]
    for number, piece in enumerate(pieces):
        pltpu.make_async_copy(piece, held.at[number], sems.at[number]).start()
    out[...] = jnp.zeros_like(out)

    @pl.loop(0, len(pieces))
    def _(number):
        pltpu.make_async_copy(pieces[0], held.at[number], sems.at[number]).wait()
        half = (number + 1) // 2
        step = jnp.where(number % 2 == 1, size - half, half)
        start = lax.rem(me + step, size) * width
        out[...] += lax.dot_general(
            held[number], weight[:, pl.ds(pl.multiple_of(start, HD), width)],
            (((1,), (1,)), ((), ())), preferred_element_type=jnp.float32,
        )


def half_body(low, high, low_out, high_out, sems):
    cut = low_out.shape[0]
    copies = (
        pltpu.make_async_copy(low.at[pl.ds(0, cut)], low_out, sems.at[0]),
        pltpu.make_async_copy(high.at[pl.ds(cut, cut)], high_out, sems.at[1]),
    )
    for copy in copies:
        copy.start()
    for copy in copies:
        copy.wait()


def grad_end_body(size, me_ref, weight, begun, from_low, from_high, low, high, out):
    me = me_ref[0]
    half = size // 2
    cut, width = low.shape

    def term(piece, step):
        start = lax.rem(me + step, size) * width
        return lax.dot_general(
            piece, weight[:, pl.ds(pl.multiple_of(start, HD), width)],
            (((1,), (1,)), ((), ())), preferred_element_type=jnp.float32,
        )

    total = begun[...] + term(from_low[...], size - half + 1) + term(from_high[...], half - 1)
    for rows, piece in ((slice(0, cut), low), (slice(cut, 2 * cut), high)):
        out[rows] = (total[rows] + term(piece[...], half)).astype(jnp.bfloat16)


def project_body(size, me_ref, attention, weight, *outs):
    me = me_ref[0]
    width = attention.shape[1]

    @pl.loop(0, attention.shape[0] // BLK)
    def _(block):
        rows = pl.ds(pl.multiple_of(block * BLK, BLK), BLK)
        for step, out in enumerate(outs):
            start = lax.rem(me + step, size) * width
            out[rows] = jnp.dot(
                attention[rows], weight[:, pl.ds(pl.multiple_of(start, HD), width)],
                preferred_element_type=jnp.float32,
            ).astype(jnp.bfloat16)


def add(*terms):
    total = terms[0].astype(jnp.float32)
    for term in terms[1:]:
        total = total + term.astype(jnp.float32)
    return total.astype(jnp.bfloat16)


def ring_pair(pair):
    size = lax.axis_size("head")
    out = []
    for x, sign in ((pair[0], 1), (pair[1], -1)):
        out.append(lax.ppermute(x, "head", [(i, (i + sign) % size) for i in range(size)]))
    return tuple(out)


def layer(queries, key_states, value_states, block_lists, out_weight, out_grad):
    size = lax.axis_size("head")
    cells, width = queries.shape
    blocks = cells // BLK
    heads = width // HD
    me = lax.axis_index("seq").reshape(1).astype(jnp.int32)
    column = lax.axis_index("head").reshape(1).astype(jnp.int32)
    bf16, f32 = jnp.bfloat16, jnp.float32
    far = 2 * blocks

    def shape(*dims, dtype=bf16):
        return jax.ShapeDtypeStruct(dims, dtype)

    def call(body, in_specs, out_shape, *operands, out_specs=None, mib=10, scratch=()):
        return pl.pallas_call(
            body,
            in_specs=in_specs,
            out_specs=out_specs or [VMEM] * len(out_shape),
            out_shape=out_shape,
            scratch_shapes=scratch,
            compiler_params=pltpu.CompilerParams(vmem_limit_bytes=mib * 1024 * 1024),
        )(*operands)

    lists = block_lists.T
    piece = shape(2, BLK, width)
    mine, other = call(
        lambda *refs: pack_body(blocks, *refs), [VMEM, SMEM, HBM, HBM], [piece, piece],
        lists, me,
        *(pltpu.with_memory_space_constraint(x, pltpu.HBM) for x in (key_states, value_states)),
        scratch=[pltpu.SemaphoreType.DMA((2, 2))],
    )
    entries = block_lists.reshape(-1)
    entry_group = jnp.arange(entries.shape[0], dtype=jnp.int32) // (blocks * K_SEL)
    far_entry = jnp.where(entries // blocks != entry_group, entries, -1)
    all_blocks = jnp.arange(block_lists.shape[0], dtype=jnp.int32)
    named = jnp.any(far_entry[None, :] == all_blocks[:, None], axis=1).astype(jnp.int32)
    ahead = jnp.concatenate([jnp.zeros((1,), jnp.int32), named[:-1]])
    ahead2 = jnp.concatenate([jnp.zeros((2,), jnp.int32), named[:-2]])
    inner = all_blocks % blocks
    ports = jnp.where(inner == 0, 0, jnp.where(inner == 1, ahead, jnp.maximum(ahead, ahead2)))

    (table,) = call(
        lambda *refs: plan_body(blocks, *refs), [SMEM] * 3,
        [shape(4 * far + 2 * blocks * K_SEL + 1, dtype=jnp.int32)], lists, ports, me, out_specs=[SMEM],
    )

    half = size // 2
    cut = cells // 2
    ring = [(out_grad, out_grad)]
    for _ in range(1, half):
        ring.append(ring_pair(ring[-1]))
    across = ring_pair(call(
        half_body, [HBM] * 2, [shape(cut, width)] * 2, *ring[-1],
        scratch=[pltpu.SemaphoreType.DMA((2,))],
    ))
    pieces = [out_grad]
    for step in range(1, half - 1):
        pieces += ring[step]

    def join(*parts):
        total = sum(part.shape[0] for part in parts)
        return call(join_body, [VMEM] * len(parts), [shape(total, BLK, width)], *parts)[0]

    base = join(mine, swap(other))
    left, right = hop(base, 0, 1), hop(base, 0, -1)
    mid_a = join(base, left)
    low_a, high_a = hop(mid_a, 1, 1), hop(mid_a, 1, -1)
    mid_b = join(right, hop(left[:2], 0, 1), hop(right[2:], 0, -1))
    low_b, high_b = hop(mid_b, 1, 1), hop(mid_b, 1, -1)
    far_a, far_b = hop(low_a, 1, 1), hop(high_b, 1, -1)
    gathered = (mid_a, low_a, high_a, far_a, mid_b, low_b, high_b, far_b)
    (picked,) = call(
        lambda *refs: pick_body(far, *refs), [SMEM] + [ANY] * 8, [shape(far, BLK, width)],
        table, *gathered, scratch=[pltpu.SemaphoreType.DMA((far,))],
    )
    swapped = swap(picked)
    (begun,) = call(
        lambda *refs: grad_body(size, *refs), [SMEM, VMEM] + [HBM] * len(pieces),
        [shape(cells, width, dtype=f32)], column, out_weight, *pieces,
        scratch=[pltpu.VMEM((len(pieces), cells, width), bf16), pltpu.SemaphoreType.DMA((len(pieces),))],
    )
    (grad_attn,) = call(
        lambda *refs: grad_end_body(size, *refs), [SMEM] + [VMEM] * 6, [shape(cells, width)],
        column, out_weight, begun, *ring[-1], *across,
    )
    attention, query_grad, near, terms, terms_other = call(
        lambda *refs: attend_body(blocks, heads, 1.0 / math.sqrt(HD), *refs),
        [SMEM, SMEM, VMEM, ANY, ANY, VMEM] + [ANY] * 9,
        [
            shape(cells, width), shape(cells, width), shape(2, cells, width, dtype=f32),
            shape(far, BLK, width), shape(far, BLK, width),
        ],
        table, me, queries, key_states, value_states, grad_attn, swapped, *gathered,
        scratch=[
            pltpu.VMEM((2, blocks, K_SEL * BLK, width), bf16),
            pltpu.VMEM((2, blocks + far, BLK, width), f32),
            pltpu.SemaphoreType.DMA((blocks, K_SEL, 2)),
        ],
        mib=16,
    )
    theirs = swap(terms_other)
    parts = call(
        lambda *refs: project_body(size, *refs), [SMEM, VMEM, VMEM], [shape(cells, width)] * size,
        column, attention, out_weight,
    )
    lead = (table, terms, theirs)
    lead_specs = [SMEM, VMEM, VMEM]
    eight = shape(8, BLK, width)
    far_low, far_high = call(lambda *refs: pair_body(3, 7, *refs), lead_specs, [eight] * 2, *lead)
    up_b, down_a = call(lambda *refs: pair_body(6, 1, *refs), lead_specs, [eight] * 2, *lead)
    from_low, from_high = hop(far_low, 1, 1), hop(far_high, 1, -1)
    low_b, high_a = hop(up_b, 1, 1), hop(down_a, 1, -1)
    ahead, back = ring_pair((parts[half][:cut], parts[half][cut:]))
    up_a, down_b = call(late_body, lead_specs + [VMEM] * 2, [eight] * 2, *lead, from_low, from_high)
    low_a, high_b = hop(up_a, 1, 1), hop(down_b, 1, -1)
    ahead = jnp.concatenate([add(parts[half - 1][:cut], ahead), parts[half - 1][cut:]])
    back = jnp.concatenate([parts[half + 1][:cut], add(parts[half + 1][cut:], back)])
    for distance in range(half - 2, -1, -1):
        ahead, back = ring_pair((ahead, back))
        if distance:
            ahead, back = add(parts[distance], ahead), add(parts[size - distance], back)
    attended = add(parts[0], ahead, back)
    far_low, far_high = call(
        opposite_body, lead_specs + [VMEM] * 2, [piece] * 2, *lead, low_b, high_b,
        scratch=[pltpu.VMEM((4, BLK, width), f32)],
    )
    own, down, up = call(
        mid_body, lead_specs + [VMEM] * 4, [shape(4, BLK, width)] * 3,
        *lead, low_a, high_a, low_b, high_b,
        scratch=[pltpu.VMEM((8, BLK, width), f32), pltpu.VMEM((4, BLK, width), f32)],
    )
    down, up = call(
        turn_body, [VMEM] * 4, [shape(4, BLK, width)] * 2,
        down, up, hop(far_low, 0, 1), hop(far_high, 0, -1),
    )
    mine, other = call(sum_body, [VMEM] * 3, [piece, piece], own, hop(up, 0, 1), hop(down, 0, -1))
    key_grad, value_grad = call(
        lambda *refs: collect_body(blocks, *refs), [SMEM, SMEM, SMEM] + [VMEM] * 3,
        [shape(cells, width)] * 2,
        ports, named, me, near, mine, swap(other),
    )
    return attended, query_grad, key_grad, value_grad


def solution(mesh):
    in_specs = (
        P("seq", "head"),
        P("seq", "head"),
        P("seq", "head"),
        P(),
        P("head", None),
        P("seq", "head"),
    )
    out_specs = (P("seq", "head"), P("seq", "head"), P("seq", "head"), P("seq", "head"))
    return jax.shard_map(layer, mesh=mesh, in_specs=in_specs, out_specs=out_specs, check_vma=False)
```

```python
import math

import jax
import jax.numpy as jnp
from jax import lax
from jax.experimental import pallas as pl
from jax.experimental.pallas import tpu as pltpu
from jax.sharding import PartitionSpec as P


HD = 128
BLK = 128
K_SEL = 4


SMEM = pl.BlockSpec(memory_space=pltpu.SMEM)
VMEM = pl.BlockSpec(memory_space=pltpu.VMEM)
ANY = pl.BlockSpec(memory_space=pl.ANY)
HBM = pl.BlockSpec(memory_space=pltpu.HBM)


NX, NY, NC = 4, 4, 2


def place_of(group):
    return group // (NY * NC), (group // NC) % NY, group % NC


def steps_of(leg, sign):
    pairs = []
    for group in range(NX * NY * NC):
        x, y, core = place_of(group)
        if (core == 0) == (leg == 0):
            x = (x + sign) % NX
        else:
            y = (y + sign) % NY
        pairs.append((group, (x * NY + y) * NC + core))
    return pairs


def swap_of():
    return [(group, group ^ 1) for group in range(NX * NY * NC)]


def hop(x, leg, sign):
    return lax.ppermute(x, "seq", steps_of(leg, sign))


def swap(x):
    return lax.ppermute(x, "seq", swap_of())


def route(me, entry, port, blocks):
    x, y, core = place_of(me)
    owner_x, owner_y, owner_core = place_of(entry // blocks)
    dx = (owner_x - x + NX) % NX
    dy = (owner_y - y + NY) % NY
    first = jnp.where(core == 0, dx, dy)
    second = jnp.where(core == 0, dy, dx)
    order = jnp.where(first == 0, 0, jnp.where(first == 3, 1, jnp.where(first == 1, 2, 3)))
    return second, order * 4 + 2 * jnp.where(owner_core == core, 0, 1) + port


def fetch(gathered, code, target, sem):
    for first in range(0, len(gathered), 4):

        @pl.when((code >= first * 16) & (code < (first + 4) * 16))
        def _():
            for kind in range(first, first + 4):

                @pl.when((code >= kind * 16) & (code < (kind + 1) * 16))
                def _():
                    pltpu.make_async_copy(gathered[kind].at[code - kind * 16], target, sem).start()


def join_body(*refs):
    out, start = refs[-1], 0
    for ref in refs[:-1]:
        out[start:start + ref.shape[0]] = ref[...]
        start += ref.shape[0]


def pack_body(blocks, lists, me_ref, key, value, mine, other, sems):
    me = me_ref[0]
    core = me % NC
    row = lax.broadcasted_iota(jnp.int32, lists.shape, 1) - me * blocks
    entry = jnp.where((row < 0) | (row >= blocks), lists[...] - me * blocks, -1)
    named = [jnp.max(jnp.where(entry == block, 1.0, 0.0)) > 0.5 for block in range(blocks)]
    first = jnp.where(named[0], 0, jnp.where(named[1], 1, 2))
    second = jnp.where(named[2], 2, jnp.where(named[1], 1, 0))
    for port, block in enumerate((first, second)):
        rows = pl.ds(pl.multiple_of(block * BLK, BLK), BLK)

        @pl.when(core == 0)
        def _():
            pltpu.make_async_copy(key.at[rows], mine.at[port], sems.at[port, 0]).start()
            pltpu.make_async_copy(value.at[rows], other.at[port], sems.at[port, 1]).start()

        @pl.when(core != 0)
        def _():
            pltpu.make_async_copy(value.at[rows], mine.at[port], sems.at[port, 0]).start()
            pltpu.make_async_copy(key.at[rows], other.at[port], sems.at[port, 1]).start()

    for port in range(2):
        rows = pl.ds(0, BLK)
        pltpu.make_async_copy(key.at[rows], mine.at[port], sems.at[port, 0]).wait()
        pltpu.make_async_copy(key.at[rows], other.at[port], sems.at[port, 1]).wait()


def plan_body(blocks, lists, ports, me_ref, table):
    me = me_ref[0]
    far_count = 2 * blocks
    steps = blocks * K_SEL
    spare = table.shape[0] - 1
    partner = me + 1 - 2 * (me % NC)
    for group_index, group in enumerate((me, partner)):
        seen = []
        for block in range(blocks):
            count = jnp.int32(2 * block)
            row = []
            for item in range(K_SEL):
                step = block * K_SEL + item
                entry = lists[item, group * blocks + block]
                place = entry - group * blocks
                far = (place < 0) | (place >= blocks)
                number = count
                distance, index = route(me, entry, ports[entry], blocks)
                kind = jnp.where(index < 8, 0, 4) + jnp.where(
                    distance == 0, 0, jnp.where(distance == 3, 1, jnp.where(distance == 1, 2, 3))
                )
                first = number
                for earlier_entry, earlier_number in reversed(seen):
                    first = jnp.where(earlier_entry == entry, earlier_number, first)
                row.append((entry, number))
                table[jnp.where(far, group_index * far_count + number, spare)] = kind * 16 + index % 8
                table[jnp.where(far, (2 + group_index) * far_count + number, spare)] = jnp.where(first == number, 1, 0)
                if group_index == 0:
                    table[4 * far_count + step] = jnp.where(far, blocks + first, place)
                    table[4 * far_count + steps + step] = jnp.where(far, number, -1)
                count = count + jnp.where(far, 1, 0)
            seen += row


def pick_body(far_count, table, *refs):
    gathered, out, sems = refs[:-2], refs[-2], refs[-1]
    for number in range(far_count):
        fetch(gathered, table[far_count + number], out.at[number], sems.at[number])
    for number in range(far_count):
        pltpu.make_async_copy(gathered[0].at[0], out.at[number], sems.at[number]).wait()


def attend_body(blocks, heads, scale, table, me_ref, query, key, value, grad, swapped, *refs):
    gathered, refs = refs[:8], refs[8:]
    attention, query_grad, near, mine, other, rows_of, totals, sems = refs
    me = me_ref[0]
    core = me % NC
    width = heads * HD
    far_count = 2 * blocks
    steps = blocks * K_SEL

    def start(step, carry):
        block, item = step // K_SEL, step % K_SEL
        slot = table[4 * far_count + step]
        number = table[4 * far_count + steps + step]
        rows = pl.ds(pl.multiple_of(item * BLK, BLK), BLK)

        @pl.when(number < 0)
        def _():
            source = pl.ds(pl.multiple_of(slot * BLK, BLK), BLK)
            pltpu.make_async_copy(key.at[source], rows_of.at[0, block, rows], sems.at[block, item, 0]).start()
            pltpu.make_async_copy(value.at[source], rows_of.at[1, block, rows], sems.at[block, item, 1]).start()

        @pl.when(number >= 0)
        def _():
            fetch(gathered, table[jnp.maximum(number, 0)], rows_of.at[core, block, rows], sems.at[block, item, core])
            pltpu.make_async_copy(
                swapped.at[jnp.maximum(number, 0)], rows_of.at[1 - core, block, rows], sems.at[block, item, 1 - core]
            ).start()

        return carry

    lax.fori_loop(0, steps, start, 0)

    @pl.loop(0, blocks + far_count)
    def _(slot):
        totals[0, slot] = jnp.zeros((BLK, width), jnp.float32)
        totals[1, slot] = jnp.zeros((BLK, width), jnp.float32)

    @pl.loop(0, blocks)
    def _(block):
        for item in range(K_SEL):
            rows = pl.ds(item * BLK, BLK)
            for kind in range(2):
                pltpu.make_async_copy(
                    key.at[pl.ds(0, BLK)], rows_of.at[kind, block, rows], sems.at[block, item, kind]
                ).wait()
        own_rows = pl.ds(pl.multiple_of(block * BLK, BLK), BLK)
        f32, bf16 = jnp.float32, jnp.bfloat16
        every = [pl.ds(head * HD, HD) for head in range(heads)]

        def rows_times_rows(left, right):
            return lax.dot_general(left, right, (((1,), (1,)), ((), ())), preferred_element_type=f32)

        def columns_times(left, right):
            return lax.dot_general(left, right, (((0,), (0,)), ((), ())), preferred_element_type=f32)

        qs = [query[own_rows, columns] for columns in every]
        gs = [grad[own_rows, columns] for columns in every]
        ks = [rows_of[0, block, :, columns] for columns in every]
        vs = [rows_of[1, block, :, columns] for columns in every]
        scores = [rows_times_rows(q, k) * scale for q, k in zip(qs, ks)]
        grad_probs = [rows_times_rows(g, v) for g, v in zip(gs, vs)]
        raised = [jnp.exp(x - jnp.max(x, axis=-1, keepdims=True)) for x in scores]
        probs = [x * (1.0 / jnp.sum(x, axis=-1, keepdims=True)) for x in raised]
        lows = [x.astype(bf16) for x in probs]
        mixed = [jnp.dot(low, v, preferred_element_type=f32).astype(bf16) for low, v in zip(lows, vs)]
        deltas = [jnp.sum(g.astype(f32) * x.astype(f32), axis=-1, keepdims=True) for g, x in zip(gs, mixed)]
        grad_scores = [(p * (x - d)).astype(bf16) for p, x, d in zip(probs, grad_probs, deltas)]
        for head, columns in enumerate(every):
            attention[own_rows, columns] = mixed[head]
            query_grad[own_rows, columns] = (
                jnp.dot(grad_scores[head], ks[head], preferred_element_type=f32) * scale
            ).astype(bf16)
        for head, columns in enumerate(every):
            key_terms = columns_times(grad_scores[head], qs[head]) * scale
            value_terms = columns_times(lows[head], gs[head])
            for item in range(K_SEL):
                slot = table[4 * far_count + block * K_SEL + item]
                part = slice(item * BLK, (item + 1) * BLK)
                totals[0, slot, :, columns] += key_terms[part]
                totals[1, slot, :, columns] += value_terms[part]

    @pl.loop(0, far_count)
    def _(number):
        mine[number] = totals[core, blocks + number].astype(jnp.bfloat16)
        other[number] = totals[1 - core, blocks + number].astype(jnp.bfloat16)

    @pl.loop(0, blocks)
    def _(block):
        rows = pl.ds(pl.multiple_of(block * BLK, BLK), BLK)
        near[0, rows] = totals[0, block]
        near[1, rows] = totals[1, block]


def add_terms(table, mine, theirs, cases):
    far_count = mine.shape[0]
    for group, terms in enumerate((mine, theirs)):

        def body(number, carry):
            code = table[group * far_count + number]
            first = table[(2 + group) * far_count + number] != 0
            for kind, low, high, ref in cases:

                @pl.when(first & (code >= kind * 16 + low) & (code < kind * 16 + high))
                def _():
                    index = code - (kind * 16 + low)

                    @pl.loop(0, 4)
                    def _(part):
                        rows = pl.ds(pl.multiple_of(part * (BLK // 4), BLK // 4), BLK // 4)
                        ref[index, rows] = (
                            ref[index, rows].astype(jnp.float32) + terms[number, rows].astype(jnp.float32)
                        ).astype(ref.dtype)

            return carry

        lax.fori_loop(0, far_count, body, 0)


def pair_body(first_kind, second_kind, table, mine, theirs, first, second):
    @pl.loop(0, 8)
    def _(index):
        for ref in (first, second):
            ref[index] = jnp.zeros(ref.shape[1:], ref.dtype)

    add_terms(table, mine, theirs, ((first_kind, 0, 8, first), (second_kind, 0, 8, second)))


def late_body(table, mine, theirs, from_low, from_high, up, down):
    @pl.loop(0, 8)
    def _(index):
        up[index] = from_low[index]
        down[index] = from_high[index]

    add_terms(table, mine, theirs, ((2, 0, 8, up), (5, 0, 8, down)))


def opposite_body(table, mine, theirs, low_second, high_second, far_low, far_high, total):
    f32, bf16 = jnp.float32, jnp.bfloat16

    @pl.loop(0, 4)
    def _(index):
        total[index] = low_second[index + 4].astype(f32) + high_second[index + 4].astype(f32)

    add_terms(table, mine, theirs, ((4, 4, 8, total),))
    for index in range(2):
        far_low[index] = total[index].astype(bf16)
        far_high[index] = total[index + 2].astype(bf16)


def mid_body(table, mine, theirs, low_first, high_first, low_second, high_second, own, down, up, first, second):
    f32, bf16 = jnp.float32, jnp.bfloat16

    @pl.loop(0, 4)
    def _(index):
        first[index] = low_first[index].astype(f32) + high_first[index].astype(f32)
        first[index + 4] = low_first[index + 4].astype(f32) + high_first[index + 4].astype(f32)
        second[index] = low_second[index].astype(f32) + high_second[index].astype(f32)

    add_terms(table, mine, theirs, ((0, 0, 8, first), (4, 0, 4, second)))

    @pl.loop(0, 4)
    def _(index):
        own[index] = first[index].astype(bf16)
        down[index] = first[index + 4].astype(bf16)
        up[index] = second[index].astype(bf16)


def turn_body(down, up, from_low, from_high, down_out, up_out):
    f32 = jnp.float32
    up_out[:2] = (up[:2].astype(f32) + from_low[...].astype(f32)).astype(jnp.bfloat16)
    up_out[2:] = up[2:]
    down_out[:2] = down[:2]
    down_out[2:] = (down[2:].astype(f32) + from_high[...].astype(f32)).astype(jnp.bfloat16)


def sum_body(own, from_low, from_high, mine, other):
    f32 = jnp.float32
    total = (own[...].astype(f32) + from_low[...].astype(f32) + from_high[...].astype(f32)).astype(jnp.bfloat16)
    mine[...] = total[:2]
    other[...] = total[2:]


def collect_body(blocks, ports, named, me_ref, near, mine, swapped, key_grad, value_grad):
    me = me_ref[0]
    core = me % NC
    f32 = jnp.float32

    @pl.loop(0, blocks)
    def _(block):
        rows = pl.ds(pl.multiple_of(block * BLK, BLK), BLK)
        port = ports[me * blocks + block]
        weight = named[me * blocks + block] != 0
        for kind, out in enumerate((key_grad, value_grad)):
            term = jnp.where(core == kind, mine[port].astype(f32), swapped[port].astype(f32))
            out[rows] = (near[kind, rows] + jnp.where(weight, term, 0.0)).astype(jnp.bfloat16)


def grad_body(size, me_ref, weight, *refs):
    pieces, (out, held, sems) = refs[:-3], refs[-3:]
    me = me_ref[0]
    width = out.shape[1]
    for number, piece in enumerate(pieces):
        pltpu.make_async_copy(piece, held.at[number], sems.at[number]).start()
    out[...] = jnp.zeros_like(out)

    @pl.loop(0, len(pieces))
    def _(number):
        pltpu.make_async_copy(pieces[0], held.at[number], sems.at[number]).wait()
        half = (number + 1) // 2
        step = jnp.where(number % 2 == 1, size - half, half)
        start = lax.rem(me + step, size) * width
        out[...] += lax.dot_general(
            held[number], weight[:, pl.ds(pl.multiple_of(start, HD), width)],
            (((1,), (1,)), ((), ())), preferred_element_type=jnp.float32,
        )


def half_body(low, high, low_out, high_out, sems):
    cut = low_out.shape[0]
    copies = (
        pltpu.make_async_copy(low.at[pl.ds(0, cut)], low_out, sems.at[0]),
        pltpu.make_async_copy(high.at[pl.ds(cut, cut)], high_out, sems.at[1]),
    )
    for copy in copies:
        copy.start()
    for copy in copies:
        copy.wait()


def grad_end_body(size, me_ref, weight, begun, from_low, from_high, low, high, out):
    me = me_ref[0]
    half = size // 2
    cut, width = low.shape

    def term(piece, step):
        start = lax.rem(me + step, size) * width
        return lax.dot_general(
            piece, weight[:, pl.ds(pl.multiple_of(start, HD), width)],
            (((1,), (1,)), ((), ())), preferred_element_type=jnp.float32,
        )

    total = begun[...] + term(from_low[...], size - half + 1) + term(from_high[...], half - 1)
    for rows, piece in ((slice(0, cut), low), (slice(cut, 2 * cut), high)):
        out[rows] = (total[rows] + term(piece[...], half)).astype(jnp.bfloat16)


def project_body(size, me_ref, attention, weight, *outs):
    me = me_ref[0]
    width = attention.shape[1]

    @pl.loop(0, attention.shape[0] // BLK)
    def _(block):
        rows = pl.ds(pl.multiple_of(block * BLK, BLK), BLK)
        for step, out in enumerate(outs):
            start = lax.rem(me + step, size) * width
            out[rows] = jnp.dot(
                attention[rows], weight[:, pl.ds(pl.multiple_of(start, HD), width)],
                preferred_element_type=jnp.float32,
            ).astype(jnp.bfloat16)


def add(*terms):
    total = terms[0].astype(jnp.float32)
    for term in terms[1:]:
        total = total + term.astype(jnp.float32)
    return total.astype(jnp.bfloat16)


def ring_pair(pair):
    size = lax.axis_size("head")
    out = []
    for x, sign in ((pair[0], 1), (pair[1], -1)):
        out.append(lax.ppermute(x, "head", [(i, (i + sign) % size) for i in range(size)]))
    return tuple(out)


def layer(queries, key_states, value_states, block_lists, out_weight, out_grad):
    size = lax.axis_size("head")
    cells, width = queries.shape
    blocks = cells // BLK
    heads = width // HD
    me = lax.axis_index("seq").reshape(1).astype(jnp.int32)
    column = lax.axis_index("head").reshape(1).astype(jnp.int32)
    bf16, f32 = jnp.bfloat16, jnp.float32
    far = 2 * blocks

    def shape(*dims, dtype=bf16):
        return jax.ShapeDtypeStruct(dims, dtype)

    def call(body, in_specs, out_shape, *operands, out_specs=None, mib=10, scratch=()):
        return pl.pallas_call(
            body,
            in_specs=in_specs,
            out_specs=out_specs or [VMEM] * len(out_shape),
            out_shape=out_shape,
            scratch_shapes=scratch,
            compiler_params=pltpu.CompilerParams(vmem_limit_bytes=mib * 1024 * 1024),
        )(*operands)

    lists = block_lists.T
    piece = shape(2, BLK, width)
    mine, other = call(
        lambda *refs: pack_body(blocks, *refs), [VMEM, SMEM, HBM, HBM], [piece, piece],
        lists, me,
        *(pltpu.with_memory_space_constraint(x, pltpu.HBM) for x in (key_states, value_states)),
        scratch=[pltpu.SemaphoreType.DMA((2, 2))],
    )
    entries = block_lists.reshape(-1)
    entry_group = jnp.arange(entries.shape[0], dtype=jnp.int32) // (blocks * K_SEL)
    far_entry = jnp.where(entries // blocks != entry_group, entries, -1)
    all_blocks = jnp.arange(block_lists.shape[0], dtype=jnp.int32)
    named = jnp.any(far_entry[None, :] == all_blocks[:, None], axis=1).astype(jnp.int32)
    ahead = jnp.concatenate([jnp.zeros((1,), jnp.int32), named[:-1]])
    ahead2 = jnp.concatenate([jnp.zeros((2,), jnp.int32), named[:-2]])
    inner = all_blocks % blocks
    ports = jnp.where(inner == 0, 0, jnp.where(inner == 1, ahead, jnp.maximum(ahead, ahead2)))

    (table,) = call(
        lambda *refs: plan_body(blocks, *refs), [SMEM] * 3,
        [shape(4 * far + 2 * blocks * K_SEL + 1, dtype=jnp.int32)], lists, ports, me, out_specs=[SMEM],
    )

    half = size // 2
    cut = cells // 2
    ring = [(out_grad, out_grad)]
    for _ in range(1, half):
        ring.append(ring_pair(ring[-1]))
    across = ring_pair(call(
        half_body, [HBM] * 2, [shape(cut, width)] * 2, *ring[-1],
        scratch=[pltpu.SemaphoreType.DMA((2,))],
    ))
    pieces = [out_grad]
    for step in range(1, half - 1):
        pieces += ring[step]

    def join(*parts):
        total = sum(part.shape[0] for part in parts)
        return call(join_body, [VMEM] * len(parts), [shape(total, BLK, width)], *parts)[0]

    base = join(mine, swap(other))
    left, right = hop(base, 0, 1), hop(base, 0, -1)
    mid_a = join(base, left)
    low_a, high_a = hop(mid_a, 1, 1), hop(mid_a, 1, -1)
    mid_b = join(right, hop(left[:2], 0, 1), hop(right[2:], 0, -1))
    low_b, high_b = hop(mid_b, 1, 1), hop(mid_b, 1, -1)
    far_a, far_b = hop(low_a, 1, 1), hop(high_b, 1, -1)
    gathered = (mid_a, low_a, high_a, far_a, mid_b, low_b, high_b, far_b)
    (picked,) = call(
        lambda *refs: pick_body(far, *refs), [SMEM] + [ANY] * 8, [shape(far, BLK, width)],
        table, *gathered, scratch=[pltpu.SemaphoreType.DMA((far,))],
    )
    swapped = swap(picked)
    (begun,) = call(
        lambda *refs: grad_body(size, *refs), [SMEM, VMEM] + [HBM] * len(pieces),
        [shape(cells, width, dtype=f32)], column, out_weight, *pieces,
        scratch=[pltpu.VMEM((len(pieces), cells, width), bf16), pltpu.SemaphoreType.DMA((len(pieces),))],
    )
    (grad_attn,) = call(
        lambda *refs: grad_end_body(size, *refs), [SMEM] + [VMEM] * 6, [shape(cells, width)],
        column, out_weight, begun, *ring[-1], *across,
    )
    attention, query_grad, near, terms, terms_other = call(
        lambda *refs: attend_body(blocks, heads, 1.0 / math.sqrt(HD), *refs),
        [SMEM, SMEM, VMEM, ANY, ANY, VMEM] + [ANY] * 9,
        [
            shape(cells, width), shape(cells, width), shape(2, cells, width, dtype=f32),
            shape(far, BLK, width), shape(far, BLK, width),
        ],
        table, me, queries, key_states, value_states, grad_attn, swapped, *gathered,
        scratch=[
            pltpu.VMEM((2, blocks, K_SEL * BLK, width), bf16),
            pltpu.VMEM((2, blocks + far, BLK, width), f32),
            pltpu.SemaphoreType.DMA((blocks, K_SEL, 2)),
        ],
        mib=16,
    )
    theirs = swap(terms_other)
    parts = call(
        lambda *refs: project_body(size, *refs), [SMEM, VMEM, VMEM], [shape(cells, width)] * size,
        column, attention, out_weight,
    )
    lead = (table, terms, theirs)
    lead_specs = [SMEM, VMEM, VMEM]
    eight = shape(8, BLK, width)
    far_low, far_high = call(lambda *refs: pair_body(3, 7, *refs), lead_specs, [eight] * 2, *lead)
    up_b, down_a = call(lambda *refs: pair_body(6, 1, *refs), lead_specs, [eight] * 2, *lead)
    from_low, from_high = hop(far_low, 1, 1), hop(far_high, 1, -1)
    low_b, high_a = hop(up_b, 1, 1), hop(down_a, 1, -1)
    ahead, back = ring_pair((parts[half][:cut], parts[half][cut:]))
    up_a, down_b = call(late_body, lead_specs + [VMEM] * 2, [eight] * 2, *lead, from_low, from_high)
    low_a, high_b = hop(up_a, 1, 1), hop(down_b, 1, -1)
    ahead = jnp.concatenate([add(parts[half - 1][:cut], ahead), parts[half - 1][cut:]])
    back = jnp.concatenate([parts[half + 1][:cut], add(parts[half + 1][cut:], back)])
    for distance in range(half - 2, -1, -1):
        ahead, back = ring_pair((ahead, back))
        if distance:
            ahead, back = add(parts[distance], ahead), add(parts[size - distance], back)
    attended = add(parts[0], ahead, back)
    far_low, far_high = call(
        opposite_body, lead_specs + [VMEM] * 2, [piece] * 2, *lead, low_b, high_b,
        scratch=[pltpu.VMEM((4, BLK, width), f32)],
    )
    own, down, up = call(
        mid_body, lead_specs + [VMEM] * 4, [shape(4, BLK, width)] * 3,
        *lead, low_a, high_a, low_b, high_b,
        scratch=[pltpu.VMEM((8, BLK, width), f32), pltpu.VMEM((4, BLK, width), f32)],
    )
    down, up = call(
        turn_body, [VMEM] * 4, [shape(4, BLK, width)] * 2,
        down, up, hop(far_low, 0, 1), hop(far_high, 0, -1),
    )
    mine, other = call(sum_body, [VMEM] * 3, [piece, piece], own, hop(up, 0, 1), hop(down, 0, -1))
    key_grad, value_grad = call(
        lambda *refs: collect_body(blocks, *refs), [SMEM, SMEM, SMEM] + [VMEM] * 3,
        [shape(cells, width)] * 2,
        ports, named, me, near, mine, swap(other),
    )
    return attended, query_grad, key_grad, value_grad


def solution(mesh):
    in_specs = (
        P("seq", "head"),
        P("seq", "head"),
        P("seq", "head"),
        P(),
        P("head", None),
        P("seq", "head"),
    )
    out_specs = (P("seq", "head"), P("seq", "head"), P("seq", "head"), P("seq", "head"))
    return jax.shard_map(layer, mesh=mesh, in_specs=in_specs, out_specs=out_specs, check_vma=False)
```
